128 devices in a mesh: row: 8 (over y, core), col: 16 (over z, x).
Axes of the slice: x: 4, y: 4, z: 4, core: 2. Of those that a mesh axis runs over, the one named last changes fastest.
Arguments:
- positions: float32 [3, 16384], P(None, 'col'), may hold values from 0 to 4
- modulus: float32 [16384], P('col'), may hold values from 0.5 to 2
- self_weight: float32 [128, 768], P('col'), may hold values from 1 to 4
- omega: float32 [128, 768, 256], P('col'), may hold values from -6 to 6
- psi: float32 [128, 768, 256], P('row'), may hold values from -6 to 6
- blocks: int32 [8, 16, 2, 2], P('row', 'col'), may hold values from -1 to 15, as said below
Outputs:
- row_basis: float32 [128, 768, 256], P('row', 'col')
- col_basis: float32 [128, 768, 256], P('col', 'row')
The draws below stay inside these ranges and needn't reach their ends.
Inputs may be any that keep to these rules, and one draw needn't show every extreme that they name: `blocks`: on every device the valid slots come first and the rest hold -1 in both entries; valid pairs are distinct, a row entry below 16, a column entry below 8, and never a cluster paired with itself; each device has at least one valid slot and some device has all 2 slots valid.
All inputs are finite; a program needn't handle non-finite values.
Results may differ from the reference program's by a relative error of at most 0.0003.
Values sent between devices are 32-bit elements; how exact they have to be, the bound alone decides.
No kernel may reach another device: no remote copies, remote signals or barrier semaphores. Data moves between devices by JAX's collectives and lax.ppermute only.
A program may use at most 192 MiB of HBM per device.

```python
import math
import jax
import jax.numpy as jnp
from jax import lax

ZC = 128
SK = 256
CL_DEV = 8
BLK_DEV = 2
CLUSTERS = 128
ROW_CL = 16
ZONES = 16384
N_ROW = 8
N_COL = 16


def draw_blocks(key, part):
    row_count = CL_DEV * N_COL // N_ROW
    col_count = CL_DEV
    devices = N_ROW * N_COL
    pair_total = row_count * col_count
    key_score = jax.random.fold_in(key, 11)
    key_light = jax.random.fold_in(key, 12)
    key_heavy = jax.random.fold_in(key, 13)
    key_full = jax.random.fold_in(key, 14)
    scores = jax.random.randint(key_score, (devices, pair_total), 0, 2 ** 20) * pair_total + jnp.arange(pair_total, dtype=jnp.int32)[None, :]
    device_ids = jnp.arange(devices, dtype=jnp.int32)
    row_dev = device_ids // N_COL
    col_dev = device_ids % N_COL
    pair_ids = jnp.arange(pair_total, dtype=jnp.int32)
    global_row = row_dev[:, None] * row_count + pair_ids[None, :] // col_count
    global_col = col_dev[:, None] * col_count + pair_ids[None, :] % col_count
    scores = jnp.where(global_row == global_col, -1, scores)
    _, chosen = lax.top_k(scores, BLK_DEV)
    light = jax.random.randint(key_light, (devices,), 1, BLK_DEV // 2 + 1)
    heavy = jax.random.randint(key_heavy, (devices,), 0, 8) == 0
    full_one = jax.random.randint(key_full, (), 0, devices)
    counts = jnp.where(heavy | (device_ids == full_one), BLK_DEV, light)
    slot_ids = jnp.arange(BLK_DEV, dtype=jnp.int32)
    live = slot_ids[None, :] < counts[:, None]
    rows_local = jnp.where(live, chosen // col_count, -1)
    cols_local = jnp.where(live, chosen % col_count, -1)
    return jnp.stack([rows_local, cols_local], axis=-1).reshape(N_ROW, N_COL, BLK_DEV, 2).astype(jnp.int32)


def block_scale(own_key, extent, pieces, smallest, high):
    level = 1.0
    for position, parts in pieces:
        steps = jax.random.uniform(jax.random.fold_in(jax.random.fold_in(own_key, 6), position), (parts,), jnp.float32, smallest / len(pieces), high / len(pieces))
        level = level * jnp.repeat(jnp.exp(steps), extent[position] // parts).reshape((-1,) + (1,) * (len(extent) - 1 - position))
    return level


def bell_draw(rng, dims, scale, most, split=(), kind=jnp.bfloat16):
    entries = scale * jax.random.normal(rng, dims, jnp.float32)
    if split:
        entries = entries * block_scale(rng, dims, split, -0.22, 0.18)
    return jnp.clip(entries, -most, most).astype(kind)


def setup_inputs(seed: int = 0) -> dict:
    keys = jax.random.split(jax.random.key(seed), 7)
    positions = jnp.clip(4.0 * jax.random.uniform(keys[0], (3, ZONES), jnp.float32) ** block_scale(keys[0], (3, ZONES), ((1, 16),), -0.2, 0.2), 0.0, 4.0)
    modulus = jnp.clip(jnp.exp(math.log(2.0) - 1.3862944 * jax.random.uniform(keys[1], (ZONES,), jnp.float32) ** block_scale(keys[1], (ZONES,), ((0, 16),), -0.2, 0.2)), 0.5, 2.0)
    self_weight = jnp.clip(jnp.exp(math.log(4.0) - 1.3862944 * jax.random.uniform(keys[2], (CLUSTERS, 6 * ZC), jnp.float32) ** block_scale(keys[2], (CLUSTERS, 6 * ZC), ((0, 16),), -0.2, 0.2)), 1.0, 4.0)
    omega = bell_draw(keys[3], (CLUSTERS, 6 * ZC, SK), 1.0, 6.0, ((0, 16),), jnp.float32)
    psi = bell_draw(keys[4], (CLUSTERS, 6 * ZC, SK), 1.0, 6.0, ((0, 8),), jnp.float32)
    blocks = draw_blocks(jax.random.fold_in(keys[6], 71), 0)
    return {"positions": positions, "modulus": modulus, "self_weight": self_weight, "omega": omega, "psi": psi, "blocks": blocks}


COUPLE = 0.25
ROOT_TWO = 1.4142135623730951
HIGH = lax.Precision.HIGHEST

def make_tiles(row_points, row_scale, col_points, col_scale):
    offsets = row_points[:, :, :, None] - col_points[:, :, None, :]
    spread = lax.optimization_barrier(jnp.sum(offsets * offsets, axis=1)) + 1.0
    inverse = lax.rsqrt(spread)
    normal = offsets * inverse[:, None]
    weight_ab = COUPLE * inverse * inverse * inverse * row_scale[:, :, None] * col_scale[:, None, :]
    comp_x = normal[:, 0]
    comp_y = normal[:, 1]
    comp_z = normal[:, 2]
    voigt = jnp.stack([comp_x * comp_x, comp_y * comp_y, comp_z * comp_z, ROOT_TWO * comp_y * comp_z, ROOT_TWO * comp_x * comp_z, ROOT_TWO * comp_x * comp_y], axis=1)
    trace_vec = jnp.array([1.0, 1.0, 1.0, 0.0, 0.0, 0.0], dtype=voigt.dtype)
    identity = jnp.eye(6, dtype=voigt.dtype)
    voigt_row = voigt[:, :, :, None, :]
    voigt_col = jnp.transpose(voigt, (0, 2, 1, 3))[:, None]
    angular = identity[None, :, None, :, None] + voigt_row * trace_vec[None, None, None, :, None] + trace_vec[None, :, None, None, None] * voigt_col - 5.0 * voigt_row * voigt_col
    result = angular * weight_ab[:, None, :, None, :]
    zones_per = row_points.shape[2]
    return result.reshape(result.shape[0], 6 * zones_per, 6 * zones_per)

def orthonormal(sketch):
    gram = jnp.einsum('kxs,kxt->kst', sketch, sketch, precision=HIGH)
    factor = jnp.linalg.cholesky(gram)
    return lax.linalg.triangular_solve(factor, sketch, left_side=False, lower=True, transpose_a=True)

def reference(positions, modulus, self_weight, omega, psi, blocks):
    points = positions.reshape(3, CLUSTERS, ZC)
    scales = modulus.reshape(CLUSTERS, ZC)
    row_base = (jnp.arange(N_ROW, dtype=jnp.int32) * ROW_CL)[:, None, None]
    col_base = (jnp.arange(N_COL, dtype=jnp.int32) * CL_DEV)[None, :, None]
    valid = blocks[..., 0] >= 0
    row_ids = jnp.where(valid, row_base + blocks[..., 0], 0).reshape(-1).astype(jnp.int32)
    col_ids = jnp.where(valid, col_base + blocks[..., 1], 0).reshape(-1).astype(jnp.int32)
    flags = valid.reshape(-1)
    start_rows = self_weight[:, :, None] * omega
    start_cols = self_weight[:, :, None] * psi

    def visit(state, entry):
        row_id, col_id, flag = entry

        def add_pair(inner):
            sketch_rows, sketch_cols = inner
            row_pts = lax.dynamic_index_in_dim(points, row_id, 1, keepdims=False)
            col_pts = lax.dynamic_index_in_dim(points, col_id, 1, keepdims=False)
            row_mod = lax.dynamic_index_in_dim(scales, row_id, 0, keepdims=False)
            col_mod = lax.dynamic_index_in_dim(scales, col_id, 0, keepdims=False)
            block = make_tiles(row_pts[None], row_mod[None], col_pts[None], col_mod[None])[0]
            omega_j = lax.dynamic_index_in_dim(omega, col_id, 0, keepdims=False)
            psi_i = lax.dynamic_index_in_dim(psi, row_id, 0, keepdims=False)
            row_term = jnp.dot(block, omega_j, precision=HIGH)
            col_term = jnp.dot(block.T, psi_i, precision=HIGH)
            return (sketch_rows.at[row_id].add(row_term), sketch_cols.at[col_id].add(col_term))
        return (lax.cond(flag, add_pair, lambda inner: inner, state), None)
    (row_sketch, col_sketch), _ = lax.scan(visit, (start_rows, start_cols), (row_ids, col_ids, flags))
    return (orthonormal(row_sketch), orthonormal(col_sketch))
```

```python
import functools
import jax
import jax.numpy as jnp
from jax import lax
from jax.experimental import pallas as pl
from jax.experimental.pallas import tpu as pltpu
from jax.sharding import PartitionSpec as P

COUPLE = 0.25
ROOT_TWO = 1.4142135623730951
HIGH = lax.Precision.HIGHEST
ZC = 128
HEIGHT = 768
SK = 256
NR = 8
NC = 16
ROW_CL = 16
COL_CL = 8
SLOTS = 2
ROW_CUT = HEIGHT // NC
COL_CUT = HEIGHT // NR
TAG = 8
BOTH = ("row", "col")
F32 = jnp.float32
BF16 = jnp.bfloat16


def device(y, core, z, x):
    return (2 * y + core) * NC + 4 * z + x


def point_routes():
    near, far = [], []
    for y in range(4):
        for core in range(2):
            for z in range(4):
                for x in range(4):
                    away = (x // 2) ^ core
                    bit = x % 2
                    target = device(y, core, z, x)
                    first = 2 * core + (bit ^ away)
                    second = 2 * core + (1 ^ bit ^ away)
                    src_y = (z + 2) % 4
                    near.append((device(src_y, away, y, first), target))
                    far.append((device(src_y, away, y, second), target))
    return near, far


def omega_route():
    route = []
    for y in range(4):
        for core in range(2):
            for z in range(4):
                for x in range(4):
                    src = device((2 * (z % 2) + x // 2 + y) % 4, x % 2, y, 2 * core + z // 2)
                    route.append((src, device(y, core, z, x)))
    return route


def psi_route():
    route = []
    for y in range(4):
        for core in range(2):
            for z in range(4):
                for x in range(4):
                    src = device(z, x // 2, (y + z) % 4, 2 * core + x % 2)
                    route.append((src, device(y, core, z, x)))
    return route


def split(value):
    high = value.astype(BF16)
    return high, (value - high.astype(F32)).astype(BF16)


def pair_kernel(meta, own_pts, near_pts, far_pts, src, out, high_t, low_t, high_w, low_w, buf, left, sem, *, cut, turned):
    pieces = HEIGHT // cut
    for slot in range(SLOTS):

        @pl.when(meta[slot, 0] >= 0)
        def _(slot=slot):
            row_id = meta[slot, 0]
            col_id = meta[slot, 1]
            pick = row_id if turned else col_id
            copy = pltpu.make_async_copy(src.at[pick], buf, sem)
            copy.start()
            row_half = row_id // COL_CL
            row_k = row_id % COL_CL
            from_near = row_half == meta[SLOTS, 0]

            def row_line(c):
                a = near_pts[c, pl.ds(row_k, 1), :]
                b = far_pts[c, pl.ds(row_k, 1), :]
                return jnp.where(from_near, a, b)

            rows = [row_line(c) for c in range(4)]
            cols = [own_pts[c, pl.ds(col_id, 1), :] for c in range(4)]
            down, across = (cols, rows) if turned else (rows, cols)
            for c in range(4):
                left[c] = jnp.transpose(jnp.broadcast_to(down[c], (ZC, ZC)))

            def chunk(step, carry):
                at = pl.multiple_of(step * 16, 16)
                wide = [jnp.broadcast_to(v, (16, ZC)) for v in across]
                tall = [left[c, pl.ds(at, 16), :] for c in range(4)]
                dx = tall[0] - wide[0]
                dy = tall[1] - wide[1]
                dz = tall[2] - wide[2]
                inv = lax.rsqrt(dx * dx + dy * dy + dz * dz + 1.0)
                w = (COUPLE * (inv * inv * inv)) * (tall[3] * wide[3])
                nx, ny, nz = dx * inv, dy * inv, dz * inv
                u = [
                    nx * nx,
                    ny * ny,
                    nz * nz,
                    ROOT_TWO * (ny * nz),
                    ROOT_TWO * (nx * nz),
                    ROOT_TWO * (nx * ny),
                ]
                v = [w * t for t in u]
                v5 = [5.0 * t for t in v]
                for p in range(6):
                    for q in range(p, 6):
                        m = -(v5[p] * u[q])
                        if q < 3:
                            m = m + (v[p] + v[q])
                        elif p < 3:
                            m = m + v[q]
                        if p == q:
                            m = m + w
                        hi, lo = split(m)
                        high_t[pl.ds(p * ZC + at, 16), q * ZC : (q + 1) * ZC] = hi
                        low_t[pl.ds(p * ZC + at, 16), q * ZC : (q + 1) * ZC] = lo
                        if p != q:
                            high_t[pl.ds(q * ZC + at, 16), p * ZC : (p + 1) * ZC] = hi
                            low_t[pl.ds(q * ZC + at, 16), p * ZC : (p + 1) * ZC] = lo
                return carry

            lax.fori_loop(0, ZC // 16, chunk, 0)
            copy.wait()
            hi, lo = split(buf[...])
            high_w[...] = hi
            low_w[...] = lo
            step_rows = cut * 2
            for g in range(HEIGHT // step_rows):
                part = pl.ds(g * step_rows, step_rows)
                acc = jnp.dot(high_t[part, :], high_w[...], preferred_element_type=F32)
                acc += jnp.dot(high_t[part, :], low_w[...], preferred_element_type=F32)
                acc += jnp.dot(low_t[part, :], high_w[...], preferred_element_type=F32)
                out[2 * g, slot * cut : (slot + 1) * cut, :] = acc[:cut]
                out[2 * g + 1, slot * cut : (slot + 1) * cut, :] = acc[cut:]

        tag = jnp.full((1, 1, SK), meta[slot, 1 if turned else 0].astype(F32))
        out[:, SLOTS * cut + slot * (TAG // SLOTS) : SLOTS * cut + (slot + 1) * (TAG // SLOTS), :] = (
            jnp.broadcast_to(tag, (pieces, TAG // SLOTS, SK))
        )


def pair_terms(meta, own_pts, near_pts, far_pts, src, cut, turned):
    pieces = HEIGHT // cut
    vmem = pl.BlockSpec(memory_space=pltpu.VMEM)
    return pl.pallas_call(
        functools.partial(pair_kernel, cut=cut, turned=turned),
        out_shape=jax.ShapeDtypeStruct((pieces, SLOTS * cut + TAG, SK), F32),
        in_specs=[pl.BlockSpec(memory_space=pltpu.SMEM), vmem, vmem, vmem, pl.BlockSpec(memory_space=pl.ANY)],
        out_specs=vmem,
        scratch_shapes=[
            pltpu.VMEM((HEIGHT, HEIGHT), BF16),
            pltpu.VMEM((HEIGHT, HEIGHT), BF16),
            pltpu.VMEM((HEIGHT, SK), BF16),
            pltpu.VMEM((HEIGHT, SK), BF16),
            pltpu.VMEM((HEIGHT, SK), F32),
            pltpu.VMEM((4, ZC, ZC), F32),
            pltpu.SemaphoreType.DMA,
        ],
        compiler_params=pltpu.CompilerParams(vmem_limit_bytes=24 << 20),
        cost_estimate=pl.CostEstimate(flops=2_000_000_000, bytes_accessed=4_000_000, transcendentals=32768),
        name="pair_cols" if turned else "pair_rows",
    )(meta, own_pts, near_pts, far_pts, src)


def add_kernel(ids, arrived, out, *, cut):
    out[...] = jnp.zeros_like(out)
    for k in range(arrived.shape[0]):
        for slot in range(SLOTS):

            @pl.when(ids[k, slot] >= 0)
            def _(k=k, slot=slot):
                out[ids[k, slot]] += arrived[k, slot * cut : (slot + 1) * cut, :]


def add_arrived(arrived, clusters, cut):
    ids = arrived[:, SLOTS * cut :: TAG // SLOTS, 0].astype(jnp.int32)
    vmem = pl.BlockSpec(memory_space=pltpu.VMEM)
    return pl.pallas_call(
        functools.partial(add_kernel, cut=cut),
        out_shape=jax.ShapeDtypeStruct((clusters, cut, SK), F32),
        in_specs=[pl.BlockSpec(memory_space=pltpu.SMEM), vmem],
        out_specs=vmem,
        compiler_params=pltpu.CompilerParams(vmem_limit_bytes=16 << 20),
        cost_estimate=pl.CostEstimate(flops=1_000_000, bytes_accessed=3_000_000, transcendentals=0),
        name="add_arrived",
    )(ids, arrived)


BLK = 64


def factor_inverse(diag):
    sub = lax.broadcasted_iota(jnp.int32, (8, 128), 0)
    lane = lax.broadcasted_iota(jnp.int32, (8, 128), 1)
    body = jnp.concatenate([diag, diag], axis=1)
    groups = []
    for g in range(BLK // 8):
        eye = jnp.where(lane == sub + 8 * g, 1.0, 0.0).astype(F32)
        groups.append(jnp.where(lane < BLK, eye, body[8 * g : 8 * g + 8]))
    done = []
    for kb in range(BLK // 8):
        at = BLK + 8 * kb
        spread = {
            g: [jnp.broadcast_to(groups[g][:, at + t : at + t + 1], (8, 128)) for t in range(8)]
            for g in range(kb, BLK // 8)
        }
        rows = [jnp.broadcast_to(groups[kb][t : t + 1, :], (8, 128)) for t in range(8)]
        e = [[jnp.broadcast_to(spread[kb][t][s : s + 1, :], (8, 128)) if s >= t else None for t in range(8)] for s in range(8)]
        final = jnp.zeros((8, 128), F32)
        for t in range(8):
            root = lax.rsqrt(e[t][t])
            inv = 1.0 / e[t][t]
            final = jnp.where(sub == t, rows[t] * root, final)
            scaled = rows[t] * inv
            for s in range(t + 1, 8):
                m = e[s][t] * inv
                for u in range(t + 1, s + 1):
                    e[s][u] = e[s][u] - m * e[u][t]
                rows[s] = rows[s] - e[s][t] * scaled
                for g in range(kb + 1, BLK // 8):
                    spread[g][s] = spread[g][s] - spread[g][t] * m
            for g in range(kb + 1, BLK // 8):
                groups[g] = groups[g] - spread[g][t] * scaled
        done.append(final)
    return jnp.concatenate(done, axis=0)[:, :BLK]


def basis_kernel(rows, self_rows, cols, self_cols, out_rows, out_cols, sk, gram, inverse):
    n = SK // BLK
    dims0 = (((0,), (0,)), ((), ()))
    for w, (got, own) in enumerate(((rows, self_rows), (cols, self_cols))):
        sk[w] = got[...] + own[...]
        gram[w] = lax.dot_general(sk[w], sk[w], dims0, precision=HIGH, preferred_element_type=F32)
        inverse[w] = jnp.zeros((SK, SK), F32)
    for k in range(n):
        here = slice(k * BLK, (k + 1) * BLK)
        low = [factor_inverse(gram[w, here, here]) for w in range(2)]
        for w in range(2):
            if k:
                inverse[w, here, : k * BLK] = jnp.dot(
                    low[w], inverse[w, here, : k * BLK], precision=HIGH, preferred_element_type=F32
                )
            inverse[w, here, here] = low[w]
            if k < n - 1:
                rest = slice((k + 1) * BLK, SK)
                upper = jnp.dot(low[w], gram[w, here, rest], precision=HIGH, preferred_element_type=F32)
                gram[w, rest, rest] = gram[w, rest, rest] - lax.dot_general(
                    upper, upper, dims0, precision=HIGH, preferred_element_type=F32
                )
                inverse[w, rest, : (k + 1) * BLK] = inverse[w, rest, : (k + 1) * BLK] - lax.dot_general(
                    upper, inverse[w, here, : (k + 1) * BLK], dims0, precision=HIGH, preferred_element_type=F32
                )
    for w, out in enumerate((out_rows, out_cols)):
        out[...] = lax.dot_general(
            sk[w], inverse[w], (((1,), (1,)), ((), ())), precision=HIGH, preferred_element_type=F32
        )


def bases(rows, self_rows, cols, self_cols):
    shape = jax.ShapeDtypeStruct((HEIGHT, SK), F32)
    vmem = pl.BlockSpec(memory_space=pltpu.VMEM)
    return pl.pallas_call(
        basis_kernel,
        out_shape=(shape, shape),
        in_specs=[vmem] * 4,
        out_specs=(vmem, vmem),
        scratch_shapes=[
            pltpu.VMEM((2, HEIGHT, SK), F32),
            pltpu.VMEM((2, SK, SK), F32),
            pltpu.VMEM((2, SK, SK), F32),
        ],
        compiler_params=pltpu.CompilerParams(vmem_limit_bytes=32 << 20),
        cost_estimate=pl.CostEstimate(flops=3_000_000_000, bytes_accessed=5_000_000, transcendentals=0),
        name="bases",
    )(rows, self_rows, cols, self_cols)


def trade(value, axis):
    return lax.all_to_all(value, axis, split_axis=0, concat_axis=0, tiled=True)


def per_device(positions, modulus, self_weight, omega, psi, blocks):
    row_at = lax.axis_index("row")
    col_at = lax.axis_index("col")
    near_route, far_route = point_routes()

    points = jnp.concatenate([positions, modulus[None]], axis=0).reshape(4, COL_CL, ZC)
    near_pts = lax.ppermute(points, BOTH, near_route)
    far_pts = lax.ppermute(points, BOTH, far_route)

    src_y, src_core, src_z, src_x = row_at // 2, row_at % 2, col_at // 4, col_at % 4
    bits = (src_y - src_z) % 4
    omega_pick = (bits // 2) * 4 + (bits % 2) * 2 + src_core
    omega_send = omega[omega_pick] * self_weight[omega_pick][:, None]
    psi_pick = (src_x % 2) * 8 + ((src_z - src_y) % 4) * 2 + src_x // 2
    psi_send = psi[psi_pick]
    omega_send, psi_send, near_pts, far_pts = lax.optimization_barrier((omega_send, psi_send, near_pts, far_pts))
    self_rows = lax.ppermute(omega_send, BOTH, omega_route())
    psi_here = lax.ppermute(psi_send, BOTH, psi_route())
    self_cols = psi_here * self_weight[row_at][:, None]

    pairs = blocks.reshape(SLOTS, 2)
    core = row_at % 2
    away = ((col_at % 4) // 2) ^ core
    near_half = (col_at % 2) ^ away
    meta = jnp.concatenate([pairs, jnp.stack([near_half, near_half])[None]], axis=0).astype(jnp.int32)

    row_terms = pair_terms(meta, points, near_pts, far_pts, omega, ROW_CUT, False)
    col_terms = pair_terms(meta, points, near_pts, far_pts, psi, COL_CUT, True)

    row_sum = add_arrived(trade(row_terms, "col"), ROW_CL, ROW_CUT)
    col_sum = add_arrived(trade(col_terms, "row"), COL_CL, COL_CUT)
    rows = trade(row_sum, "col").reshape(HEIGHT, SK)
    cols = trade(col_sum, "row").reshape(HEIGHT, SK)
    row_q, col_q = bases(rows, self_rows, cols, self_cols)
    row_basis = trade(row_q.reshape(NC, ROW_CUT, SK), "col")
    col_basis = trade(col_q.reshape(NR, COL_CUT, SK), "row")
    return (row_basis, col_basis)


def solution(mesh):
    placed = (
        P(None, "col"),
        P("col"),
        P("col", None),
        P("col", None, None),
        P("row", None, None),
        P("row", "col", None, None),
    )
    return jax.shard_map(
        per_device,
        mesh=mesh,
        in_specs=placed,
        out_specs=(P("row", "col", None), P("col", "row", None)),
        check_vma=False,
    )
```

```python
import functools
import jax
import jax.numpy as jnp
from jax import lax
from jax.experimental import pallas as pl
from jax.experimental.pallas import tpu as pltpu
from jax.sharding import PartitionSpec as P

COUPLE = 0.25
ROOT_TWO = 1.4142135623730951
HIGH = lax.Precision.HIGHEST
ZC = 128
HEIGHT = 768
SK = 256
NR = 8
NC = 16
ROW_CL = 16
COL_CL = 8
SLOTS = 2
ROW_CUT = HEIGHT // NC
COL_CUT = HEIGHT // NR
TAG = 8
BOTH = ("row", "col")
F32 = jnp.float32
BF16 = jnp.bfloat16


def device(y, core, z, x):
    return (2 * y + core) * NC + 4 * z + x


def point_routes():
    near, far = [], []
    for y in range(4):
        for core in range(2):
            for z in range(4):
                for x in range(4):
                    away = (x // 2) ^ core
                    bit = x % 2
                    target = device(y, core, z, x)
                    first = 2 * core + (bit ^ away)
                    second = 2 * core + (1 ^ bit ^ away)
                    src_y = (z + 2) % 4
                    near.append((device(src_y, away, y, first), target))
                    far.append((device(src_y, away, y, second), target))
    return near, far


def omega_routes(turn):
    inside, along = [], []
    for y in range(4):
        for core in range(2):
            for z in range(4):
                for x in range(4):
                    src_y = y ^ (2 * (x // 2) + z % 2) ^ turn
                    src_core = core ^ (x % 2)
                    middle = device(src_y, src_core, z, x)
                    inside.append((device(src_y, src_core, y, 2 * core + z // 2), middle))
                    along.append((middle, device(y, core, z, x)))
    return inside, along


def psi_route():
    route = []
    for y in range(4):
        for core in range(2):
            for z in range(4):
                for x in range(4):
                    src = device(z, x // 2, (y + z) % 4, 2 * core + x % 2)
                    route.append((src, device(y, core, z, x)))
    return route


def split(value):
    high = value.astype(BF16)
    return high, (value - high.astype(F32)).astype(BF16)


def pair_kernel(meta, own_pts, near_pts, far_pts, src, *refs, cut, turned):
    pieces = HEIGHT // cut
    outs, refs = (refs[:pieces], refs[pieces:]) if turned else ((), refs)
    out, high_t, low_t, high_w, low_w, buf, left, sem = refs[:8]

    def visit(slot, outer):
        @pl.when(meta[slot, 0] >= 0)
        def _():
            row_id = meta[slot, 0]
            col_id = meta[slot, 1]
            pick = row_id if turned else col_id
            copy = pltpu.make_async_copy(src.at[pick], buf, sem)
            copy.start()
            row_half = row_id // COL_CL
            row_k = row_id % COL_CL
            from_near = row_half == meta[SLOTS, 0]

            def row_line(c):
                a = near_pts[c, pl.ds(row_k, 1), :]
                b = far_pts[c, pl.ds(row_k, 1), :]
                return jnp.where(from_near, a, b)

            rows = [row_line(c) for c in range(4)]
            cols = [own_pts[c, pl.ds(col_id, 1), :] for c in range(4)]
            down, across = (cols, rows) if turned else (rows, cols)
            for c in range(4):
                left[c] = jnp.transpose(jnp.broadcast_to(down[c], (ZC, ZC)))

            def chunk(step, carry):
                at = pl.multiple_of(step * 16, 16)
                wide = [jnp.broadcast_to(v, (16, ZC)) for v in across]
                tall = [left[c, pl.ds(at, 16), :] for c in range(4)]
                dx = tall[0] - wide[0]
                dy = tall[1] - wide[1]
                dz = tall[2] - wide[2]
                inv = lax.rsqrt(dx * dx + dy * dy + dz * dz + 1.0)
                w = (COUPLE * (inv * inv * inv)) * (tall[3] * wide[3])
                nx, ny, nz = dx * inv, dy * inv, dz * inv
                u = [
                    nx * nx,
                    ny * ny,
                    nz * nz,
                    ROOT_TWO * (ny * nz),
                    ROOT_TWO * (nx * nz),
                    ROOT_TWO * (nx * ny),
                ]
                v = [w * t for t in u]
                v5 = [5.0 * t for t in v]
                for p in range(6):
                    for q in range(p, 6):
                        m = -(v5[p] * u[q])
                        if q < 3:
                            m = m + (v[p] + v[q])
                        elif p < 3:
                            m = m + v[q]
                        if p == q:
                            m = m + w
                        hi, lo = split(m)
                        high_t[pl.ds(p * ZC + at, 16), q * ZC : (q + 1) * ZC] = hi
                        low_t[pl.ds(p * ZC + at, 16), q * ZC : (q + 1) * ZC] = lo
                        if p != q:
                            high_t[pl.ds(q * ZC + at, 16), p * ZC : (p + 1) * ZC] = hi
                            low_t[pl.ds(q * ZC + at, 16), p * ZC : (p + 1) * ZC] = lo
                return carry

            lax.fori_loop(0, ZC // 16, chunk, 0)
            copy.wait()
            hi, lo = split(buf[...])
            high_w[...] = hi
            low_w[...] = lo
            step_rows = cut * 2

            def rows_of(g, carry):
                part = pl.ds(pl.multiple_of(g * step_rows, step_rows), step_rows)
                acc = jnp.dot(high_t[part, :], high_w[...], preferred_element_type=F32)
                acc += jnp.dot(high_t[part, :], low_w[...], preferred_element_type=F32)
                acc += jnp.dot(low_t[part, :], high_w[...], preferred_element_type=F32)
                for h in range(2):
                    out[(2 * g + h) ^ meta[SLOTS, 1], pl.ds(pl.multiple_of(slot * cut, cut), cut), :] = acc[h * cut : (h + 1) * cut]
                return carry

            lax.fori_loop(0, HEIGHT // step_rows, rows_of, 0)

        return outer

    lax.fori_loop(0, SLOTS, visit, 0)
    for slot in range(SLOTS):
        tag = jnp.full((1, 1, SK), meta[slot, 1 if turned else 0].astype(F32))
        out[:, SLOTS * cut + slot * (TAG // SLOTS) : SLOTS * cut + (slot + 1) * (TAG // SLOTS), :] = (
            jnp.broadcast_to(tag, (pieces, TAG // SLOTS, SK))
        )
    send_out(out, outs, refs[8:])


def send_out(held, outs, sems):
    copies = [pltpu.make_async_copy(held.at[k], one.at[0], sems[0].at[k]) for k, one in enumerate(outs)]
    for copy in copies:
        copy.start()
    for copy in copies:
        copy.wait()


def pair_terms(meta, own_pts, near_pts, far_pts, src, cut, turned):
    pieces = HEIGHT // cut
    vmem = pl.BlockSpec(memory_space=pltpu.VMEM)
    rows = SLOTS * cut + TAG
    if turned:
        shape = tuple(jax.ShapeDtypeStruct((1, rows, SK), F32) for _ in range(pieces))
        specs = tuple(pl.BlockSpec(memory_space=pltpu.HBM) for _ in range(pieces))
        held, sems = [pltpu.VMEM((pieces, rows, SK), F32)], [pltpu.SemaphoreType.DMA((pieces,))]
    else:
        shape, specs, held, sems = jax.ShapeDtypeStruct((pieces, rows, SK), F32), vmem, [], []
    return pl.pallas_call(
        functools.partial(pair_kernel, cut=cut, turned=turned),
        out_shape=shape,
        in_specs=[pl.BlockSpec(memory_space=pltpu.SMEM), vmem, vmem, vmem, pl.BlockSpec(memory_space=pltpu.HBM)],
        out_specs=specs,
        scratch_shapes=held
        + [
            pltpu.VMEM((HEIGHT, HEIGHT), BF16),
            pltpu.VMEM((HEIGHT, HEIGHT), BF16),
            pltpu.VMEM((HEIGHT, SK), BF16),
            pltpu.VMEM((HEIGHT, SK), BF16),
            pltpu.VMEM((HEIGHT, SK), F32),
            pltpu.VMEM((4, ZC, ZC), F32),
            pltpu.SemaphoreType.DMA,
        ]
        + sems,
        cost_estimate=pl.CostEstimate(flops=2_000_000_000, bytes_accessed=4_000_000, transcendentals=32768),
        name="pair_cols" if turned else "pair_rows",
    )(meta, own_pts, near_pts, far_pts, src)


def add_kernel(ids, turn, *refs, cut, parts):
    arrived, outs, refs = refs[:parts], refs[parts : 2 * parts], refs[2 * parts :]
    if parts == 1:
        outs, refs = (), outs + refs
    out, stage, sems = refs[:3]
    total = ids.shape[0] * SLOTS

    def fetch(at, n):
        k, slot = n // SLOTS, n % SLOTS
        if parts == 1:
            src = arrived[0].at[k, pl.ds(slot * cut, cut)]
        else:
            src = arrived[k].at[0, pl.ds(slot * cut, cut)]
        return pltpu.make_async_copy(src, stage.at[at], sems.at[at])

    for n in range(total):

        @pl.when(ids[n // SLOTS, n % SLOTS] >= 0)
        def _(n=n):
            fetch(n, n).start()

    out[...] = jnp.zeros_like(out)
    for n in range(total):

        @pl.when(ids[n // SLOTS, n % SLOTS] >= 0)
        def _(n=n):
            fetch(n, n).wait()
            out[ids[n // SLOTS, n % SLOTS] ^ turn[0]] += stage[n]

    send_out(out, outs, refs[3:])


def add_arrived(arrived, turn, clusters, cut):
    ids = [part[:, SLOTS * cut :: TAG // SLOTS, 0] for part in arrived]
    ids = jnp.concatenate(ids, axis=0).astype(jnp.int32)
    total = ids.shape[0] * SLOTS
    smem = pl.BlockSpec(memory_space=pltpu.SMEM)
    if len(arrived) > 1:
        shape = tuple(jax.ShapeDtypeStruct((1, cut, SK), F32) for _ in range(clusters))
        specs = tuple(pl.BlockSpec(memory_space=pltpu.HBM) for _ in range(clusters))
        held, sems = [pltpu.VMEM((clusters, cut, SK), F32)], [pltpu.SemaphoreType.DMA((clusters,))]
    else:
        shape, held, sems = jax.ShapeDtypeStruct((clusters, cut, SK), F32), [], []
        specs = pl.BlockSpec(memory_space=pltpu.VMEM)
    return pl.pallas_call(
        functools.partial(add_kernel, cut=cut, parts=len(arrived)),
        out_shape=shape,
        in_specs=[smem, smem] + [pl.BlockSpec(memory_space=pltpu.HBM)] * len(arrived),
        out_specs=specs,
        scratch_shapes=held + [pltpu.VMEM((total, cut, SK), F32), pltpu.SemaphoreType.DMA((total,))] + sems,
        cost_estimate=pl.CostEstimate(flops=1_000_000, bytes_accessed=3_000_000, transcendentals=0),
        name="add_arrived",
    )(ids, turn.reshape(1), *arrived)


BLK = 64


def factor_inverse(diag):
    sub = lax.broadcasted_iota(jnp.int32, (8, 128), 0)
    lane = lax.broadcasted_iota(jnp.int32, (8, 128), 1)
    body = jnp.concatenate([diag, diag], axis=1)
    groups = []
    for g in range(BLK // 8):
        eye = jnp.where(lane == sub + 8 * g, 1.0, 0.0).astype(F32)
        groups.append(jnp.where(lane < BLK, eye, body[8 * g : 8 * g + 8]))
    done = []
    for kb in range(BLK // 8):
        at = BLK + 8 * kb
        spread = {
            g: [jnp.broadcast_to(groups[g][:, at + t : at + t + 1], (8, 128)) for t in range(8)]
            for g in range(kb, BLK // 8)
        }
        rows = [jnp.broadcast_to(groups[kb][t : t + 1, :], (8, 128)) for t in range(8)]
        e = [[jnp.broadcast_to(spread[kb][t][s : s + 1, :], (8, 128)) if s >= t else None for t in range(8)] for s in range(8)]
        final = jnp.zeros((8, 128), F32)
        for t in range(8):
            root = lax.rsqrt(e[t][t])
            inv = 1.0 / e[t][t]
            final = jnp.where(sub == t, rows[t] * root, final)
            scaled = rows[t] * inv
            for s in range(t + 1, 8):
                m = e[s][t] * inv
                for u in range(t + 1, s + 1):
                    e[s][u] = e[s][u] - m * e[u][t]
                rows[s] = rows[s] - e[s][t] * scaled
                for g in range(kb + 1, BLK // 8):
                    spread[g][s] = spread[g][s] - spread[g][t] * m
            for g in range(kb + 1, BLK // 8):
                groups[g] = groups[g] - spread[g][t] * scaled
        done.append(final)
    return jnp.concatenate(done, axis=0)[:, :BLK]


def basis_kernel(turn, rows, self_high, self_low, self_cols, *refs):
    cols = refs[:NR]
    out_rows, out_cols, (sk, gram, inverse, low_q) = refs[NR], refs[NR + 1 : 2 * NR + 1], refs[2 * NR + 1 :]
    n = SK // BLK
    dims0 = (((0,), (0,)), ((), ()))
    half = HEIGHT // 2
    sk[0, :half] = rows[:half] + self_high[...]
    sk[0, half:] = rows[half:] + self_low[...]
    for k in range(NR):
        part = pl.ds(pl.multiple_of((k ^ turn[0]) * COL_CUT, COL_CUT), COL_CUT)
        sk[1, part, :] = cols[k][0] + self_cols[part, :]
    for w in range(2):
        gram[w] = lax.dot_general(sk[w], sk[w], dims0, precision=HIGH, preferred_element_type=F32)
        inverse[w] = jnp.zeros((SK, SK), F32)
    for k in range(n):
        here = slice(k * BLK, (k + 1) * BLK)
        low = [factor_inverse(gram[w, here, here]) for w in range(2)]
        for w in range(2):
            if k:
                inverse[w, here, : k * BLK] = jnp.dot(
                    low[w], inverse[w, here, : k * BLK], precision=HIGH, preferred_element_type=F32
                )
            inverse[w, here, here] = low[w]
            if k < n - 1:
                rest = slice((k + 1) * BLK, SK)
                upper = jnp.dot(low[w], gram[w, here, rest], precision=HIGH, preferred_element_type=F32)
                gram[w, rest, rest] = gram[w, rest, rest] - lax.dot_general(
                    upper, upper, dims0, precision=HIGH, preferred_element_type=F32
                )
                inverse[w, rest, : (k + 1) * BLK] = inverse[w, rest, : (k + 1) * BLK] - lax.dot_general(
                    upper, inverse[w, here, : (k + 1) * BLK], dims0, precision=HIGH, preferred_element_type=F32
                )
    dims1 = (((1,), (1,)), ((), ()))
    q = lax.dot_general(sk[1], inverse[1], dims1, precision=HIGH, preferred_element_type=F32)
    for g in range(NR):
        low_q[g ^ turn[0]] = q[g * COL_CUT : (g + 1) * COL_CUT]
    for k in range(NR):
        out_cols[k][0] = low_q[k]
    out_rows[...] = lax.dot_general(sk[0], inverse[0], dims1, precision=HIGH, preferred_element_type=F32)


def bases(turn, rows, self_rows, cols, self_cols):
    shape = jax.ShapeDtypeStruct((HEIGHT, SK), F32)
    shape_c = jax.ShapeDtypeStruct((1, COL_CUT, SK), F32)
    vmem = pl.BlockSpec(memory_space=pltpu.VMEM)
    return pl.pallas_call(
        basis_kernel,
        out_shape=(shape,) + (shape_c,) * NR,
        in_specs=[pl.BlockSpec(memory_space=pltpu.SMEM)] + [vmem] * (4 + NR),
        out_specs=(vmem,) * (NR + 1),
        scratch_shapes=[
            pltpu.VMEM((2, HEIGHT, SK), F32),
            pltpu.VMEM((2, SK, SK), F32),
            pltpu.VMEM((2, SK, SK), F32),
            pltpu.VMEM((NR, COL_CUT, SK), F32),
        ],
        compiler_params=pltpu.CompilerParams(vmem_limit_bytes=32 << 20),
        cost_estimate=pl.CostEstimate(flops=3_000_000_000, bytes_accessed=5_000_000, transcendentals=0),
        name="bases",
    )(turn.reshape(1), rows, *self_rows, self_cols, *cols)


def trade(value, axis):
    return lax.all_to_all(value, axis, split_axis=0, concat_axis=0, tiled=True)


def swap_rows(value):
    got = [value[0]]
    for k in range(1, NR):
        got.append(lax.ppermute(value[k], "row", [(i, i ^ k) for i in range(NR)]))
    return got


def level(positions, modulus, self_weight, omega, psi, blocks):
    row_at = lax.axis_index("row")
    col_at = lax.axis_index("col")
    near_route, far_route = point_routes()

    points = jnp.concatenate([positions, modulus[None]], axis=0).reshape(4, COL_CL, ZC)
    near_pts = lax.ppermute(points, BOTH, near_route)
    far_pts = lax.ppermute(points, BOTH, far_route)

    src_y, src_core, src_z, src_x = row_at // 2, row_at % 2, col_at // 4, col_at % 4
    bits = src_z ^ src_y
    omega_pick = (bits % 2) * 4 + (bits // 2) * 2 + ((src_x // 2) ^ src_core)
    half = HEIGHT // 2
    self_rows = []
    for h, turn in enumerate((0, 2)):
        inside, along = omega_routes(turn)
        pick = omega_pick ^ turn
        weight = lax.dynamic_slice(self_weight, (pick, h * half), (1, half)).reshape(half, 1)
        part = lax.dynamic_slice(omega, (pick, h * half, 0), (1, half, SK)).reshape(half, SK) * weight
        part = lax.ppermute(part, BOTH, inside)
        self_rows.append(lax.ppermute(part, BOTH, along))
    psi_pick = (src_x % 2) * 8 + ((src_z - src_y) % 4) * 2 + src_x // 2
    psi_here = lax.ppermute(psi[psi_pick], BOTH, psi_route())
    self_cols = psi_here * self_weight[row_at][:, None]

    pairs = blocks.reshape(SLOTS, 2)
    away = ((col_at % 4) // 2) ^ (row_at % 2)
    near_half = (col_at % 2) ^ away
    none = jnp.int32(0)
    row_meta = jnp.concatenate([pairs, jnp.stack([near_half, none])[None]], axis=0).astype(jnp.int32)
    col_meta = jnp.concatenate([pairs, jnp.stack([near_half, row_at])[None]], axis=0).astype(jnp.int32)

    row_terms = pair_terms(row_meta, points, near_pts, far_pts, omega, ROW_CUT, False)
    col_terms = pair_terms(col_meta, points, near_pts, far_pts, psi, COL_CUT, True)

    row_got = trade(row_terms, "col")
    col_got = swap_rows(col_terms)
    row_sum = add_arrived([row_got], none, ROW_CL, ROW_CUT)
    col_sum = add_arrived(col_got, row_at, COL_CL, COL_CUT)
    rows = trade(row_sum, "col").reshape(HEIGHT, SK)
    cols = swap_rows(col_sum)
    row_q, *col_q = bases(row_at, rows, self_rows, cols, self_cols)
    row_basis = trade(row_q.reshape(NC, ROW_CUT, SK), "col")
    col_basis = jnp.zeros((NR, COL_CUT, SK), F32)
    for k, part in enumerate(swap_rows(col_q)):
        col_basis = lax.dynamic_update_slice_in_dim(col_basis, part, row_at ^ k, 0)
    return (row_basis, col_basis)


def solution(mesh):
    placed = (
        P(None, "col"),
        P("col"),
        P("col", None),
        P("col", None, None),
        P("row", None, None),
        P("row", "col", None, None),
    )
    return jax.shard_map(
        level,
        mesh=mesh,
        in_specs=placed,
        out_specs=(P("row", "col", None), P("col", "row", None)),
        check_vma=False,
    )
```

```python
import functools
import jax
import jax.numpy as jnp
from jax import lax
from jax.experimental import pallas as pl
from jax.experimental.pallas import tpu as pltpu
from jax.sharding import PartitionSpec as P

COUPLE = 0.25
ROOT_TWO = 1.4142135623730951
HIGH = lax.Precision.HIGHEST
ZC = 128
HEIGHT = 768
SK = 256
NR = 8
NC = 16
ROW_CL = 16
COL_CL = 8
SLOTS = 2
ROW_CUT = HEIGHT // NC
COL_CUT = HEIGHT // NR
TAG = 8
BOTH = ("row", "col")
F32 = jnp.float32
BF16 = jnp.bfloat16


def device(y, core, z, x):
    return (2 * y + core) * NC + 4 * z + x


def point_routes():
    near, far = [], []
    for y in range(4):
        for core in range(2):
            for z in range(4):
                for x in range(4):
                    away = (x // 2) ^ core
                    bit = x % 2
                    target = device(y, core, z, x)
                    first = 2 * core + (bit ^ away)
                    second = 2 * core + (1 ^ bit ^ away)
                    src_y = (z + 2) % 4
                    near.append((device(src_y, away, y, first), target))
                    far.append((device(src_y, away, y, second), target))
    return near, far


def omega_routes():
    inside, along = [], []
    for y in range(4):
        for core in range(2):
            for z in range(4):
                for x in range(4):
                    src_y = y ^ (2 * (x // 2) + z % 2)
                    src_core = core ^ (x % 2)
                    middle = device(src_y, src_core, z, x)
                    inside.append((device(src_y, src_core, y, 2 * core + z // 2), middle))
                    along.append((middle, device(y, core, z, x)))
    return inside, along


def psi_route():
    route = []
    for y in range(4):
        for core in range(2):
            for z in range(4):
                for x in range(4):
                    src = device(z, x // 2, (y + z) % 4, 2 * core + x % 2)
                    route.append((src, device(y, core, z, x)))
    return route


def split(value):
    high = value.astype(BF16)
    return high, (value - high.astype(F32)).astype(BF16)


def pair_kernel(meta, own_pts, near_pts, far_pts, src, *refs, cut, turned):
    pieces = HEIGHT // cut
    outs, refs = (refs[:pieces], refs[pieces:]) if turned else ((), refs)
    out, high_t, low_t, high_w, low_w, buf, left, sem = refs[:8]

    def visit(slot, outer):
        @pl.when(meta[slot, 0] >= 0)
        def _():
            row_id = meta[slot, 0]
            col_id = meta[slot, 1]
            pick = row_id if turned else col_id
            copy = pltpu.make_async_copy(src.at[pick], buf, sem)
            copy.start()
            row_half = row_id // COL_CL
            row_k = row_id % COL_CL
            from_near = row_half == meta[SLOTS, 0]

            def row_line(c):
                a = near_pts[c, pl.ds(row_k, 1), :]
                b = far_pts[c, pl.ds(row_k, 1), :]
                return jnp.where(from_near, a, b)

            rows = [row_line(c) for c in range(4)]
            cols = [own_pts[c, pl.ds(col_id, 1), :] for c in range(4)]
            down, across = (cols, rows) if turned else (rows, cols)
            for c in range(4):
                left[c] = jnp.transpose(jnp.broadcast_to(down[c], (ZC, ZC)))

            def chunk(step, carry):
                at = pl.multiple_of(step * 16, 16)
                wide = [jnp.broadcast_to(v, (16, ZC)) for v in across]
                tall = [left[c, pl.ds(at, 16), :] for c in range(4)]
                dx = tall[0] - wide[0]
                dy = tall[1] - wide[1]
                dz = tall[2] - wide[2]
                inv = lax.rsqrt(dx * dx + dy * dy + dz * dz + 1.0)
                w = (COUPLE * (inv * inv * inv)) * (tall[3] * wide[3])
                nx, ny, nz = dx * inv, dy * inv, dz * inv
                u = [
                    nx * nx,
                    ny * ny,
                    nz * nz,
                    ROOT_TWO * (ny * nz),
                    ROOT_TWO * (nx * nz),
                    ROOT_TWO * (nx * ny),
                ]
                v = [w * t for t in u]
                v5 = [5.0 * t for t in v]
                for p in range(6):
                    for q in range(p, 6):
                        m = -(v5[p] * u[q])
                        if q < 3:
                            m = m + (v[p] + v[q])
                        elif p < 3:
                            m = m + v[q]
                        if p == q:
                            m = m + w
                        hi, lo = split(m)
                        high_t[pl.ds(p * ZC + at, 16), q * ZC : (q + 1) * ZC] = hi
                        low_t[pl.ds(p * ZC + at, 16), q * ZC : (q + 1) * ZC] = lo
                        if p != q:
                            high_t[pl.ds(q * ZC + at, 16), p * ZC : (p + 1) * ZC] = hi
                            low_t[pl.ds(q * ZC + at, 16), p * ZC : (p + 1) * ZC] = lo
                return carry

            lax.fori_loop(0, ZC // 16, chunk, 0)
            copy.wait()
            hi, lo = split(buf[...])
            high_w[...] = hi
            low_w[...] = lo
            step_rows = cut * 2

            def rows_of(g, carry):
                part = pl.ds(pl.multiple_of(g * step_rows, step_rows), step_rows)
                acc = jnp.dot(high_t[part, :], high_w[...], preferred_element_type=F32)
                acc += jnp.dot(high_t[part, :], low_w[...], preferred_element_type=F32)
                acc += jnp.dot(low_t[part, :], high_w[...], preferred_element_type=F32)
                for h in range(2):
                    out[(2 * g + h) ^ meta[SLOTS, 1], pl.ds(pl.multiple_of(slot * cut, cut), cut), :] = acc[h * cut : (h + 1) * cut]
                return carry

            lax.fori_loop(0, HEIGHT // step_rows, rows_of, 0)

        return outer

    lax.fori_loop(0, SLOTS, visit, 0)
    for slot in range(SLOTS):
        tag = jnp.full((1, 1, SK), meta[slot, 1 if turned else 0].astype(F32))
        out[:, SLOTS * cut + slot * (TAG // SLOTS) : SLOTS * cut + (slot + 1) * (TAG // SLOTS), :] = (
            jnp.broadcast_to(tag, (pieces, TAG // SLOTS, SK))
        )
    send_out(out, outs, refs[8:])


def send_out(held, outs, sems):
    copies = [pltpu.make_async_copy(held.at[k], one.at[0], sems[0].at[k]) for k, one in enumerate(outs)]
    for copy in copies:
        copy.start()
    for copy in copies:
        copy.wait()


def pair_terms(meta, own_pts, near_pts, far_pts, src, cut, turned):
    pieces = HEIGHT // cut
    vmem = pl.BlockSpec(memory_space=pltpu.VMEM)
    rows = SLOTS * cut + TAG
    if turned:
        shape = tuple(jax.ShapeDtypeStruct((1, rows, SK), F32) for _ in range(pieces))
        specs = tuple(pl.BlockSpec(memory_space=pltpu.HBM) for _ in range(pieces))
        held, sems = [pltpu.VMEM((pieces, rows, SK), F32)], [pltpu.SemaphoreType.DMA((pieces,))]
    else:
        shape, specs, held, sems = jax.ShapeDtypeStruct((pieces, rows, SK), F32), vmem, [], []
    return pl.pallas_call(
        functools.partial(pair_kernel, cut=cut, turned=turned),
        out_shape=shape,
        in_specs=[pl.BlockSpec(memory_space=pltpu.SMEM), vmem, vmem, vmem, pl.BlockSpec(memory_space=pltpu.HBM)],
        out_specs=specs,
        scratch_shapes=held
        + [
            pltpu.VMEM((HEIGHT, HEIGHT), BF16),
            pltpu.VMEM((HEIGHT, HEIGHT), BF16),
            pltpu.VMEM((HEIGHT, SK), BF16),
            pltpu.VMEM((HEIGHT, SK), BF16),
            pltpu.VMEM((HEIGHT, SK), F32),
            pltpu.VMEM((4, ZC, ZC), F32),
            pltpu.SemaphoreType.DMA,
        ]
        + sems,
        cost_estimate=pl.CostEstimate(flops=2_000_000_000, bytes_accessed=4_000_000, transcendentals=32768),
        name="pair_cols" if turned else "pair_rows",
    )(meta, own_pts, near_pts, far_pts, src)


def add_kernel(turn, *refs, cut, parts):
    arrived, outs, refs = refs[:parts], refs[parts : 2 * parts], refs[2 * parts :]
    if parts == 1:
        outs, refs = (), outs + refs
    out, stage, sems = refs[:3]
    total = stage.shape[0]
    copies = [
        pltpu.make_async_copy(arrived[0].at[k] if parts == 1 else arrived[k].at[0], stage.at[k], sems.at[k])
        for k in range(total)
    ]
    for copy in copies:
        copy.start()
    out[...] = jnp.zeros_like(out)
    for k in range(total):
        copies[k].wait()
        tags = stage[k, SLOTS * cut : SLOTS * cut + TAG, :128]
        for slot in range(SLOTS):
            pick = jnp.max(tags[slot * (TAG // SLOTS) : (slot + 1) * (TAG // SLOTS)]).astype(jnp.int32)

            @pl.when(pick >= 0)
            def _(k=k, slot=slot, pick=pick):
                out[pick ^ turn[0]] += stage[k, slot * cut : (slot + 1) * cut, :]

    send_out(out, outs, refs[3:])


def add_arrived(arrived, turn, clusters, cut):
    total = sum(part.shape[0] for part in arrived)
    smem = pl.BlockSpec(memory_space=pltpu.SMEM)
    if len(arrived) > 1:
        shape = tuple(jax.ShapeDtypeStruct((1, cut, SK), F32) for _ in range(clusters))
        specs = tuple(pl.BlockSpec(memory_space=pltpu.HBM) for _ in range(clusters))
        held, sems = [pltpu.VMEM((clusters, cut, SK), F32)], [pltpu.SemaphoreType.DMA((clusters,))]
    else:
        shape, held, sems = jax.ShapeDtypeStruct((clusters, cut, SK), F32), [], []
        specs = pl.BlockSpec(memory_space=pltpu.VMEM)
    return pl.pallas_call(
        functools.partial(add_kernel, cut=cut, parts=len(arrived)),
        out_shape=shape,
        in_specs=[smem] + [pl.BlockSpec(memory_space=pltpu.HBM)] * len(arrived),
        out_specs=specs,
        scratch_shapes=held
        + [pltpu.VMEM((total, SLOTS * cut + TAG, SK), F32), pltpu.SemaphoreType.DMA((total,))]
        + sems,
        cost_estimate=pl.CostEstimate(flops=1_000_000, bytes_accessed=3_000_000, transcendentals=0),
        name="add_arrived",
    )(turn.reshape(1), *arrived)


BLK = 64


def factor_inverse(diag):
    sub = lax.broadcasted_iota(jnp.int32, (8, 128), 0)
    lane = lax.broadcasted_iota(jnp.int32, (8, 128), 1)
    body = jnp.concatenate([diag, diag], axis=1)
    groups = []
    for g in range(BLK // 8):
        eye = jnp.where(lane == sub + 8 * g, 1.0, 0.0).astype(F32)
        groups.append(jnp.where(lane < BLK, eye, body[8 * g : 8 * g + 8]))
    done = []
    for kb in range(BLK // 8):
        at = BLK + 8 * kb
        spread = {
            g: [jnp.broadcast_to(groups[g][:, at + t : at + t + 1], (8, 128)) for t in range(8)]
            for g in range(kb, BLK // 8)
        }
        rows = [jnp.broadcast_to(groups[kb][t : t + 1, :], (8, 128)) for t in range(8)]
        e = [[jnp.broadcast_to(spread[kb][t][s : s + 1, :], (8, 128)) if s >= t else None for t in range(8)] for s in range(8)]
        final = jnp.zeros((8, 128), F32)
        for t in range(8):
            root = lax.rsqrt(e[t][t])
            inv = 1.0 / e[t][t]
            final = jnp.where(sub == t, rows[t] * root, final)
            scaled = rows[t] * inv
            for s in range(t + 1, 8):
                m = e[s][t] * inv
                for u in range(t + 1, s + 1):
                    e[s][u] = e[s][u] - m * e[u][t]
                rows[s] = rows[s] - e[s][t] * scaled
                for g in range(kb + 1, BLK // 8):
                    spread[g][s] = spread[g][s] - spread[g][t] * m
            for g in range(kb + 1, BLK // 8):
                groups[g] = groups[g] - spread[g][t] * scaled
        done.append(final)
    return jnp.concatenate(done, axis=0)[:, :BLK]


def basis_kernel(turn, rows, self_rows, self_cols, *refs):
    cols = refs[:NR]
    out_rows, out_cols = refs[NR], refs[NR + 1 : 2 * NR + 1]
    sk, sk_high, sk_low, gram, inverse, low_q = refs[2 * NR + 1 :]
    n = SK // BLK
    dims0 = (((0,), (0,)), ((), ()))
    sk[0] = rows[...] + self_rows[...]
    for k in range(NR):
        part = pl.ds(pl.multiple_of((k ^ turn[0]) * COL_CUT, COL_CUT), COL_CUT)
        sk[1, part, :] = cols[k][0] + self_cols[part, :]
    for w in range(2):
        hi, lo = split(sk[w])
        sk_high[w] = hi
        sk_low[w] = lo
        cross = lax.dot_general(sk_high[w], sk_low[w], dims0, preferred_element_type=F32)
        gram[w] = lax.dot_general(sk_high[w], sk_high[w], dims0, preferred_element_type=F32) + (cross + cross.T)
        inverse[w] = jnp.zeros((SK, SK), F32)
    for k in range(n):
        here = slice(k * BLK, (k + 1) * BLK)
        low = [factor_inverse(gram[w, here, here]) for w in range(2)]
        for w in range(2):
            if k:
                inverse[w, here, : k * BLK] = jnp.dot(
                    low[w], inverse[w, here, : k * BLK], precision=HIGH, preferred_element_type=F32
                )
            inverse[w, here, here] = low[w]
            if k < n - 1:
                rest = slice((k + 1) * BLK, SK)
                upper = jnp.dot(low[w], gram[w, here, rest], precision=HIGH, preferred_element_type=F32)
                gram[w, rest, rest] = gram[w, rest, rest] - lax.dot_general(
                    upper, upper, dims0, precision=HIGH, preferred_element_type=F32
                )
                inverse[w, rest, : (k + 1) * BLK] = inverse[w, rest, : (k + 1) * BLK] - lax.dot_general(
                    upper, inverse[w, here, : (k + 1) * BLK], dims0, precision=HIGH, preferred_element_type=F32
                )
    dims1 = (((1,), (1,)), ((), ()))

    def product(w):
        hi, lo = split(inverse[w])
        q = lax.dot_general(sk_high[w], hi, dims1, preferred_element_type=F32)
        q += lax.dot_general(sk_high[w], lo, dims1, preferred_element_type=F32)
        return q + lax.dot_general(sk_low[w], hi, dims1, preferred_element_type=F32)

    q = product(1)
    for g in range(NR):
        low_q[g ^ turn[0]] = q[g * COL_CUT : (g + 1) * COL_CUT]
    for k in range(NR):
        out_cols[k][0] = low_q[k]
    out_rows[...] = product(0)


def bases(turn, rows, self_rows, cols, self_cols):
    shape = jax.ShapeDtypeStruct((HEIGHT, SK), F32)
    shape_c = jax.ShapeDtypeStruct((1, COL_CUT, SK), F32)
    vmem = pl.BlockSpec(memory_space=pltpu.VMEM)
    return pl.pallas_call(
        basis_kernel,
        out_shape=(shape,) + (shape_c,) * NR,
        in_specs=[pl.BlockSpec(memory_space=pltpu.SMEM)] + [vmem] * (3 + NR),
        out_specs=(vmem,) * (NR + 1),
        scratch_shapes=[
            pltpu.VMEM((2, HEIGHT, SK), F32),
            pltpu.VMEM((2, HEIGHT, SK), BF16),
            pltpu.VMEM((2, HEIGHT, SK), BF16),
            pltpu.VMEM((2, SK, SK), F32),
            pltpu.VMEM((2, SK, SK), F32),
            pltpu.VMEM((NR, COL_CUT, SK), F32),
        ],
        compiler_params=pltpu.CompilerParams(vmem_limit_bytes=32 << 20),
        cost_estimate=pl.CostEstimate(flops=3_000_000_000, bytes_accessed=5_000_000, transcendentals=0),
        name="bases",
    )(turn.reshape(1), rows, self_rows, self_cols, *cols)


def trade(value, axis):
    return lax.all_to_all(value, axis, split_axis=0, concat_axis=0, tiled=True)


def swap_rows(value):
    got = [value[0]]
    for k in range(1, NR):
        got.append(lax.ppermute(value[k], "row", [(i, i ^ k) for i in range(NR)]))
    return got


def level(positions, modulus, self_weight, omega, psi, blocks):
    row_at = lax.axis_index("row")
    col_at = lax.axis_index("col")
    near_route, far_route = point_routes()

    points = jnp.concatenate([positions, modulus[None]], axis=0).reshape(4, COL_CL, ZC)
    near_pts = lax.ppermute(points, BOTH, near_route)
    far_pts = lax.ppermute(points, BOTH, far_route)

    src_y, src_core, src_z, src_x = row_at // 2, row_at % 2, col_at // 4, col_at % 4
    bits = src_z ^ src_y
    omega_pick = (bits % 2) * 4 + (bits // 2) * 2 + ((src_x // 2) ^ src_core)
    inside, along = omega_routes()
    weighted = omega[omega_pick] * self_weight[omega_pick][:, None]
    weighted = lax.ppermute(weighted, BOTH, inside)
    self_rows = lax.ppermute(weighted, BOTH, along)
    psi_pick = (src_x % 2) * 8 + ((src_z - src_y) % 4) * 2 + src_x // 2
    psi_here = lax.ppermute(psi[psi_pick], BOTH, psi_route())
    self_cols = psi_here * self_weight[row_at][:, None]

    pairs = blocks.reshape(SLOTS, 2)
    away = ((col_at % 4) // 2) ^ (row_at % 2)
    near_half = (col_at % 2) ^ away
    none = jnp.int32(0)
    row_meta = jnp.concatenate([pairs, jnp.stack([near_half, none])[None]], axis=0).astype(jnp.int32)
    col_meta = jnp.concatenate([pairs, jnp.stack([near_half, row_at])[None]], axis=0).astype(jnp.int32)

    row_terms = pair_terms(row_meta, points, near_pts, far_pts, omega, ROW_CUT, False)
    col_terms = pair_terms(col_meta, points, near_pts, far_pts, psi, COL_CUT, True)

    row_got = trade(row_terms, "col")
    col_got = swap_rows(col_terms)
    row_sum = add_arrived([row_got], none, ROW_CL, ROW_CUT)
    col_sum = add_arrived(col_got, row_at, COL_CL, COL_CUT)
    rows = trade(row_sum, "col").reshape(HEIGHT, SK)
    cols = swap_rows(col_sum)
    row_q, *col_q = bases(row_at, rows, self_rows, cols, self_cols)
    row_basis = trade(row_q.reshape(NC, ROW_CUT, SK), "col")
    col_basis = jnp.zeros((NR, COL_CUT, SK), F32)
    for k, part in enumerate(swap_rows(col_q)):
        col_basis = lax.dynamic_update_slice_in_dim(col_basis, part, row_at ^ k, 0)
    return (row_basis, col_basis)


def solution(mesh):
    placed = (
        P(None, "col"),
        P("col"),
        P("col", None),
        P("col", None, None),
        P("row", None, None),
        P("row", "col", None, None),
    )
    return jax.shard_map(
        level,
        mesh=mesh,
        in_specs=placed,
        out_specs=(P("row", "col", None), P("col", "row", None)),
        check_vma=False,
    )
```

```python
import functools
import jax
import jax.numpy as jnp
from jax import lax
from jax.experimental import pallas as pl
from jax.experimental.pallas import tpu as pltpu
from jax.sharding import PartitionSpec as P

COUPLE = 0.25
ROOT_TWO = 1.4142135623730951
HIGH = lax.Precision.HIGHEST
ZC = 128
HEIGHT = 768
SK = 256
NR = 8
NC = 16
ROW_CL = 16
COL_CL = 8
SLOTS = 2
ROW_CUT = HEIGHT // NC
COL_CUT = HEIGHT // NR
TAG = 8
BOTH = ("row", "col")
F32 = jnp.float32
BF16 = jnp.bfloat16


def device(y, core, z, x):
    return (2 * y + core) * NC + 4 * z + x


def point_routes():
    near, far = [], []
    for y in range(4):
        for core in range(2):
            for z in range(4):
                for x in range(4):
                    away = (x // 2) ^ core
                    bit = x % 2
                    target = device(y, core, z, x)
                    first = 2 * core + (bit ^ away)
                    second = 2 * core + (1 ^ bit ^ away)
                    src_y = (z + 2) % 4
                    near.append((device(src_y, away, y, first), target))
                    far.append((device(src_y, away, y, second), target))
    return near, far


def omega_routes(turn):
    inside, along = [], []
    for y in range(4):
        for core in range(2):
            for z in range(4):
                for x in range(4):
                    src_y = y ^ (2 * (x // 2) + z % 2) ^ turn
                    src_core = core ^ (x % 2)
                    middle = device(src_y, src_core, z, x)
                    inside.append((device(src_y, src_core, y, 2 * core + z // 2), middle))
                    along.append((middle, device(y, core, z, x)))
    return inside, along


def psi_route():
    route = []
    for y in range(4):
        for core in range(2):
            for z in range(4):
                for x in range(4):
                    src = device(z, x // 2, (y + z) % 4, 2 * core + x % 2)
                    route.append((src, device(y, core, z, x)))
    return route


def split(value):
    high = value.astype(BF16)
    return high, (value - high.astype(F32)).astype(BF16)


def pair_kernel(meta, own_pts, near_pts, far_pts, src, *refs, cut, turned):
    pieces = HEIGHT // cut
    outs, refs = (refs[:pieces], refs[pieces:]) if turned else ((), refs)
    out, high_t, low_t, high_w, low_w, buf, left, sem = refs[:8]

    def visit(slot, outer):
        @pl.when(meta[slot, 0] >= 0)
        def _():
            row_id = meta[slot, 0]
            col_id = meta[slot, 1]
            pick = row_id if turned else col_id
            copy = pltpu.make_async_copy(src.at[pick], buf, sem)
            copy.start()
            row_half = row_id // COL_CL
            row_k = row_id % COL_CL
            from_near = row_half == meta[SLOTS, 0]

            def row_line(c):
                a = near_pts[c, pl.ds(row_k, 1), :]
                b = far_pts[c, pl.ds(row_k, 1), :]
                return jnp.where(from_near, a, b)

            rows = [row_line(c) for c in range(4)]
            cols = [own_pts[c, pl.ds(col_id, 1), :] for c in range(4)]
            down, across = (cols, rows) if turned else (rows, cols)
            for c in range(4):
                left[c] = jnp.transpose(jnp.broadcast_to(down[c], (ZC, ZC)))

            def chunk(step, carry):
                at = pl.multiple_of(step * 16, 16)
                wide = [jnp.broadcast_to(v, (16, ZC)) for v in across]
                tall = [left[c, pl.ds(at, 16), :] for c in range(4)]
                dx = tall[0] - wide[0]
                dy = tall[1] - wide[1]
                dz = tall[2] - wide[2]
                inv = lax.rsqrt(dx * dx + dy * dy + dz * dz + 1.0)
                w = (COUPLE * (inv * inv * inv)) * (tall[3] * wide[3])
                nx, ny, nz = dx * inv, dy * inv, dz * inv
                u = [
                    nx * nx,
                    ny * ny,
                    nz * nz,
                    ROOT_TWO * (ny * nz),
                    ROOT_TWO * (nx * nz),
                    ROOT_TWO * (nx * ny),
                ]
                v = [w * t for t in u]
                v5 = [5.0 * t for t in v]
                for p in range(6):
                    for q in range(p, 6):
                        m = -(v5[p] * u[q])
                        if q < 3:
                            m = m + (v[p] + v[q])
                        elif p < 3:
                            m = m + v[q]
                        if p == q:
                            m = m + w
                        hi, lo = split(m)
                        high_t[pl.ds(p * ZC + at, 16), q * ZC : (q + 1) * ZC] = hi
                        low_t[pl.ds(p * ZC + at, 16), q * ZC : (q + 1) * ZC] = lo
                        if p != q:
                            high_t[pl.ds(q * ZC + at, 16), p * ZC : (p + 1) * ZC] = hi
                            low_t[pl.ds(q * ZC + at, 16), p * ZC : (p + 1) * ZC] = lo
                return carry

            lax.fori_loop(0, ZC // 16, chunk, 0)
            copy.wait()
            hi, lo = split(buf[...])
            high_w[...] = hi
            low_w[...] = lo
            step_rows = cut * 2

            def rows_of(g, carry):
                part = pl.ds(pl.multiple_of(g * step_rows, step_rows), step_rows)
                acc = jnp.dot(high_t[part, :], high_w[...], preferred_element_type=F32)
                acc += jnp.dot(high_t[part, :], low_w[...], preferred_element_type=F32)
                acc += jnp.dot(low_t[part, :], high_w[...], preferred_element_type=F32)
                for h in range(2):
                    out[(2 * g + h) ^ meta[SLOTS, 1], pl.ds(pl.multiple_of(slot * cut, cut), cut), :] = acc[h * cut : (h + 1) * cut]
                return carry

            lax.fori_loop(0, HEIGHT // step_rows, rows_of, 0)

        return outer

    lax.fori_loop(0, SLOTS, visit, 0)
    for slot in range(SLOTS):
        tag = jnp.full((1, 1, SK), meta[slot, 1 if turned else 0].astype(F32))
        out[:, SLOTS * cut + slot * (TAG // SLOTS) : SLOTS * cut + (slot + 1) * (TAG // SLOTS), :] = (
            jnp.broadcast_to(tag, (pieces, TAG // SLOTS, SK))
        )
    send_out(out, outs, refs[8:])


def send_out(held, outs, sems):
    copies = [pltpu.make_async_copy(held.at[k], one.at[0], sems[0].at[k]) for k, one in enumerate(outs)]
    for copy in copies:
        copy.start()
    for copy in copies:
        copy.wait()


def pair_terms(meta, own_pts, near_pts, far_pts, src, cut, turned):
    pieces = HEIGHT // cut
    vmem = pl.BlockSpec(memory_space=pltpu.VMEM)
    rows = SLOTS * cut + TAG
    if turned:
        shape = tuple(jax.ShapeDtypeStruct((1, rows, SK), F32) for _ in range(pieces))
        specs = tuple(pl.BlockSpec(memory_space=pltpu.HBM) for _ in range(pieces))
        held, sems = [pltpu.VMEM((pieces, rows, SK), F32)], [pltpu.SemaphoreType.DMA((pieces,))]
    else:
        shape, specs, held, sems = jax.ShapeDtypeStruct((pieces, rows, SK), F32), vmem, [], []
    return pl.pallas_call(
        functools.partial(pair_kernel, cut=cut, turned=turned),
        out_shape=shape,
        in_specs=[pl.BlockSpec(memory_space=pltpu.SMEM), vmem, vmem, vmem, pl.BlockSpec(memory_space=pltpu.HBM)],
        out_specs=specs,
        scratch_shapes=held
        + [
            pltpu.VMEM((HEIGHT, HEIGHT), BF16),
            pltpu.VMEM((HEIGHT, HEIGHT), BF16),
            pltpu.VMEM((HEIGHT, SK), BF16),
            pltpu.VMEM((HEIGHT, SK), BF16),
            pltpu.VMEM((HEIGHT, SK), F32),
            pltpu.VMEM((4, ZC, ZC), F32),
            pltpu.SemaphoreType.DMA,
        ]
        + sems,
        cost_estimate=pl.CostEstimate(flops=2_000_000_000, bytes_accessed=4_000_000, transcendentals=32768),
        name="pair_cols" if turned else "pair_rows",
    )(meta, own_pts, near_pts, far_pts, src)


def add_rows_kernel(ids, arrived, out, stage, sems, *, cut):
    total = ids.shape[0] * SLOTS

    def fetch(at, n):
        k, slot = n // SLOTS, n % SLOTS
        src = arrived.at[k, pl.ds(slot * cut, cut)]
        return pltpu.make_async_copy(src, stage.at[at], sems.at[at])

    for n in range(total):

        @pl.when(ids[n // SLOTS, n % SLOTS] >= 0)
        def _(n=n):
            fetch(n, n).start()

    out[...] = jnp.zeros_like(out)
    for n in range(total):

        @pl.when(ids[n // SLOTS, n % SLOTS] >= 0)
        def _(n=n):
            fetch(n, n).wait()
            out[ids[n // SLOTS, n % SLOTS]] += stage[n]


def add_rows(arrived, clusters, cut):
    ids = arrived[:, SLOTS * cut :: TAG // SLOTS, 0].astype(jnp.int32)
    total = ids.shape[0] * SLOTS
    return pl.pallas_call(
        functools.partial(add_rows_kernel, cut=cut),
        out_shape=jax.ShapeDtypeStruct((clusters, cut, SK), F32),
        in_specs=[pl.BlockSpec(memory_space=pltpu.SMEM), pl.BlockSpec(memory_space=pltpu.HBM)],
        out_specs=pl.BlockSpec(memory_space=pltpu.VMEM),
        scratch_shapes=[pltpu.VMEM((total, cut, SK), F32), pltpu.SemaphoreType.DMA((total,))],
        cost_estimate=pl.CostEstimate(flops=1_000_000, bytes_accessed=3_000_000, transcendentals=0),
        name="add_rows",
    )(ids, arrived)


def add_kernel(turn, *refs, cut, parts):
    arrived, outs, refs = refs[:parts], refs[parts : 2 * parts], refs[2 * parts :]
    if parts == 1:
        outs, refs = (), outs + refs
    out, stage, sems = refs[:3]
    total = stage.shape[0]
    copies = [
        pltpu.make_async_copy(arrived[0].at[k] if parts == 1 else arrived[k].at[0], stage.at[k], sems.at[k])
        for k in range(total)
    ]
    for copy in copies:
        copy.start()
    out[...] = jnp.zeros_like(out)
    for k in range(total):
        copies[k].wait()
        tags = stage[k, SLOTS * cut : SLOTS * cut + TAG, :128]
        for slot in range(SLOTS):
            pick = jnp.max(tags[slot * (TAG // SLOTS) : (slot + 1) * (TAG // SLOTS)]).astype(jnp.int32)

            @pl.when(pick >= 0)
            def _(k=k, slot=slot, pick=pick):
                out[pick ^ turn[0]] += stage[k, slot * cut : (slot + 1) * cut, :]

    send_out(out, outs, refs[3:])


def add_arrived(arrived, turn, clusters, cut):
    total = sum(part.shape[0] for part in arrived)
    smem = pl.BlockSpec(memory_space=pltpu.SMEM)
    if len(arrived) > 1:
        shape = tuple(jax.ShapeDtypeStruct((1, cut, SK), F32) for _ in range(clusters))
        specs = tuple(pl.BlockSpec(memory_space=pltpu.HBM) for _ in range(clusters))
        held, sems = [pltpu.VMEM((clusters, cut, SK), F32)], [pltpu.SemaphoreType.DMA((clusters,))]
    else:
        shape, held, sems = jax.ShapeDtypeStruct((clusters, cut, SK), F32), [], []
        specs = pl.BlockSpec(memory_space=pltpu.VMEM)
    return pl.pallas_call(
        functools.partial(add_kernel, cut=cut, parts=len(arrived)),
        out_shape=shape,
        in_specs=[smem] + [pl.BlockSpec(memory_space=pltpu.HBM)] * len(arrived),
        out_specs=specs,
        scratch_shapes=held
        + [pltpu.VMEM((total, SLOTS * cut + TAG, SK), F32), pltpu.SemaphoreType.DMA((total,))]
        + sems,
        cost_estimate=pl.CostEstimate(flops=1_000_000, bytes_accessed=3_000_000, transcendentals=0),
        name="add_arrived",
    )(turn.reshape(1), *arrived)


BLK = 64


def factor_inverse(diag):
    sub = lax.broadcasted_iota(jnp.int32, (8, 128), 0)
    lane = lax.broadcasted_iota(jnp.int32, (8, 128), 1)
    body = jnp.concatenate([diag, diag], axis=1)
    groups = []
    for g in range(BLK // 8):
        eye = jnp.where(lane == sub + 8 * g, 1.0, 0.0).astype(F32)
        groups.append(jnp.where(lane < BLK, eye, body[8 * g : 8 * g + 8]))
    done = []
    for kb in range(BLK // 8):
        at = BLK + 8 * kb
        spread = {
            g: [jnp.broadcast_to(groups[g][:, at + t : at + t + 1], (8, 128)) for t in range(8)]
            for g in range(kb, BLK // 8)
        }
        rows = [jnp.broadcast_to(groups[kb][t : t + 1, :], (8, 128)) for t in range(8)]
        e = [[jnp.broadcast_to(spread[kb][t][s : s + 1, :], (8, 128)) if s >= t else None for t in range(8)] for s in range(8)]
        final = jnp.zeros((8, 128), F32)
        for t in range(8):
            root = lax.rsqrt(e[t][t])
            inv = 1.0 / e[t][t]
            final = jnp.where(sub == t, rows[t] * root, final)
            scaled = rows[t] * inv
            for s in range(t + 1, 8):
                m = e[s][t] * inv
                for u in range(t + 1, s + 1):
                    e[s][u] = e[s][u] - m * e[u][t]
                rows[s] = rows[s] - e[s][t] * scaled
                for g in range(kb + 1, BLK // 8):
                    spread[g][s] = spread[g][s] - spread[g][t] * m
            for g in range(kb + 1, BLK // 8):
                groups[g] = groups[g] - spread[g][t] * scaled
        done.append(final)
    return jnp.concatenate(done, axis=0)[:, :BLK]


def basis_kernel(turn, rows, self_high, self_low, self_cols, *refs):
    cols = refs[:NR]
    out_rows, out_cols = refs[NR], refs[NR + 1 : 2 * NR + 1]
    sk, sk_high, sk_low, gram, inverse, low_q = refs[2 * NR + 1 :]
    n = SK // BLK
    dims0 = (((0,), (0,)), ((), ()))
    half = HEIGHT // 2
    sk[0, :half] = rows[:half] + self_high[...]
    sk[0, half:] = rows[half:] + self_low[...]
    for k in range(NR):
        part = pl.ds(pl.multiple_of((k ^ turn[0]) * COL_CUT, COL_CUT), COL_CUT)
        sk[1, part, :] = cols[k][0] + self_cols[part, :]
    for w in range(2):
        hi, lo = split(sk[w])
        sk_high[w] = hi
        sk_low[w] = lo
        cross = lax.dot_general(sk_high[w], sk_low[w], dims0, preferred_element_type=F32)
        gram[w] = lax.dot_general(sk_high[w], sk_high[w], dims0, preferred_element_type=F32) + (cross + cross.T)
        inverse[w] = jnp.zeros((SK, SK), F32)
    for k in range(n):
        here = slice(k * BLK, (k + 1) * BLK)
        low = [factor_inverse(gram[w, here, here]) for w in range(2)]
        for w in range(2):
            if k:
                inverse[w, here, : k * BLK] = jnp.dot(
                    low[w], inverse[w, here, : k * BLK], precision=HIGH, preferred_element_type=F32
                )
            inverse[w, here, here] = low[w]
            if k < n - 1:
                rest = slice((k + 1) * BLK, SK)
                upper = jnp.dot(low[w], gram[w, here, rest], precision=HIGH, preferred_element_type=F32)
                gram[w, rest, rest] = gram[w, rest, rest] - lax.dot_general(
                    upper, upper, dims0, precision=HIGH, preferred_element_type=F32
                )
                inverse[w, rest, : (k + 1) * BLK] = inverse[w, rest, : (k + 1) * BLK] - lax.dot_general(
                    upper, inverse[w, here, : (k + 1) * BLK], dims0, precision=HIGH, preferred_element_type=F32
                )
    dims1 = (((1,), (1,)), ((), ()))

    def product(w):
        hi, lo = split(inverse[w])
        q = lax.dot_general(sk_high[w], hi, dims1, preferred_element_type=F32)
        q += lax.dot_general(sk_high[w], lo, dims1, preferred_element_type=F32)
        return q + lax.dot_general(sk_low[w], hi, dims1, preferred_element_type=F32)

    q = product(1)
    for g in range(NR):
        low_q[g ^ turn[0]] = q[g * COL_CUT : (g + 1) * COL_CUT]
    for k in range(NR):
        out_cols[k][0] = low_q[k]
    out_rows[...] = product(0)


def bases(turn, rows, self_rows, cols, self_cols):
    shape = jax.ShapeDtypeStruct((HEIGHT, SK), F32)
    shape_c = jax.ShapeDtypeStruct((1, COL_CUT, SK), F32)
    vmem = pl.BlockSpec(memory_space=pltpu.VMEM)
    return pl.pallas_call(
        basis_kernel,
        out_shape=(shape,) + (shape_c,) * NR,
        in_specs=[pl.BlockSpec(memory_space=pltpu.SMEM)] + [vmem] * (4 + NR),
        out_specs=(vmem,) * (NR + 1),
        scratch_shapes=[
            pltpu.VMEM((2, HEIGHT, SK), F32),
            pltpu.VMEM((2, HEIGHT, SK), BF16),
            pltpu.VMEM((2, HEIGHT, SK), BF16),
            pltpu.VMEM((2, SK, SK), F32),
            pltpu.VMEM((2, SK, SK), F32),
            pltpu.VMEM((NR, COL_CUT, SK), F32),
        ],
        compiler_params=pltpu.CompilerParams(vmem_limit_bytes=32 << 20),
        cost_estimate=pl.CostEstimate(flops=3_000_000_000, bytes_accessed=5_000_000, transcendentals=0),
        name="bases",
    )(turn.reshape(1), rows, *self_rows, self_cols, *cols)


def trade(value, axis):
    return lax.all_to_all(value, axis, split_axis=0, concat_axis=0, tiled=True)


def swap_rows(value):
    got = [value[0]]
    for k in range(1, NR):
        got.append(lax.ppermute(value[k], "row", [(i, i ^ k) for i in range(NR)]))
    return got


def level(positions, modulus, self_weight, omega, psi, blocks):
    row_at = lax.axis_index("row")
    col_at = lax.axis_index("col")
    near_route, far_route = point_routes()

    points = jnp.concatenate([positions, modulus[None]], axis=0).reshape(4, COL_CL, ZC)
    near_pts = lax.ppermute(points, BOTH, near_route)
    far_pts = lax.ppermute(points, BOTH, far_route)

    src_y, src_core, src_z, src_x = row_at // 2, row_at % 2, col_at // 4, col_at % 4
    bits = src_z ^ src_y
    omega_pick = (bits % 2) * 4 + (bits // 2) * 2 + ((src_x // 2) ^ src_core)
    half = HEIGHT // 2
    self_rows = []
    for h, turn in enumerate((0, 2)):
        inside, along = omega_routes(turn)
        pick = omega_pick ^ turn
        weight = lax.dynamic_slice(self_weight, (pick, h * half), (1, half)).reshape(half, 1)
        part = lax.dynamic_slice(omega, (pick, h * half, 0), (1, half, SK)).reshape(half, SK) * weight
        part = lax.ppermute(part, BOTH, inside)
        self_rows.append(lax.ppermute(part, BOTH, along))
    psi_pick = (src_x % 2) * 8 + ((src_z - src_y) % 4) * 2 + src_x // 2
    psi_here = lax.ppermute(psi[psi_pick], BOTH, psi_route())
    self_cols = psi_here * self_weight[row_at][:, None]

    pairs = blocks.reshape(SLOTS, 2)
    away = ((col_at % 4) // 2) ^ (row_at % 2)
    near_half = (col_at % 2) ^ away
    none = jnp.int32(0)
    row_meta = jnp.concatenate([pairs, jnp.stack([near_half, none])[None]], axis=0).astype(jnp.int32)
    col_meta = jnp.concatenate([pairs, jnp.stack([near_half, row_at])[None]], axis=0).astype(jnp.int32)

    row_terms = pair_terms(row_meta, points, near_pts, far_pts, omega, ROW_CUT, False)
    col_terms = pair_terms(col_meta, points, near_pts, far_pts, psi, COL_CUT, True)

    row_got = trade(row_terms, "col")
    col_got = swap_rows(col_terms)
    row_sum = add_rows(row_got, ROW_CL, ROW_CUT)
    col_sum = add_arrived(col_got, row_at, COL_CL, COL_CUT)
    rows = trade(row_sum, "col").reshape(HEIGHT, SK)
    cols = swap_rows(col_sum)
    row_q, *col_q = bases(row_at, rows, self_rows, cols, self_cols)
    row_basis = trade(row_q.reshape(NC, ROW_CUT, SK), "col")
    col_basis = jnp.zeros((NR, COL_CUT, SK), F32)
    for k, part in enumerate(swap_rows(col_q)):
        col_basis = lax.dynamic_update_slice_in_dim(col_basis, part, row_at ^ k, 0)
    return (row_basis, col_basis)


def solution(mesh):
    placed = (
        P(None, "col"),
        P("col"),
        P("col", None),
        P("col", None, None),
        P("row", None, None),
        P("row", "col", None, None),
    )
    return jax.shard_map(
        level,
        mesh=mesh,
        in_specs=placed,
        out_specs=(P("row", "col", None), P("col", "row", None)),
        check_vma=False,
    )
```

```python
import functools
import jax
import jax.numpy as jnp
from jax import lax
from jax.experimental import pallas as pl
from jax.experimental.pallas import tpu as pltpu
from jax.sharding import PartitionSpec as P

COUPLE = 0.25
ROOT_TWO = 1.4142135623730951
HIGH = lax.Precision.HIGHEST
ZC = 128
HEIGHT = 768
SK = 256
NR = 8
NC = 16
ROW_CL = 16
COL_CL = 8
SLOTS = 2
ROW_CUT = HEIGHT // NC
COL_CUT = HEIGHT // NR
TAG = 8
BOTH = ("row", "col")
F32 = jnp.float32
BF16 = jnp.bfloat16


def device(y, core, z, x):
    return (2 * y + core) * NC + 4 * z + x


def point_routes():
    near, far = [], []
    for y in range(4):
        for core in range(2):
            for z in range(4):
                for x in range(4):
                    away = (x // 2) ^ core
                    bit = x % 2
                    target = device(y, core, z, x)
                    first = 2 * core + (bit ^ away)
                    second = 2 * core + (1 ^ bit ^ away)
                    src_y = (z + 2) % 4
                    near.append((device(src_y, away, y, first), target))
                    far.append((device(src_y, away, y, second), target))
    return near, far


def omega_routes(turn):
    inside, along = [], []
    for y in range(4):
        for core in range(2):
            for z in range(4):
                for x in range(4):
                    src_y = y ^ (2 * (x // 2) + z % 2) ^ turn
                    src_core = core ^ (x % 2)
                    middle = device(src_y, src_core, z, x)
                    inside.append((device(src_y, src_core, y, 2 * core + z // 2), middle))
                    along.append((middle, device(y, core, z, x)))
    return inside, along


def psi_route():
    route = []
    for y in range(4):
        for core in range(2):
            for z in range(4):
                for x in range(4):
                    src = device(z, x // 2, (y + z) % 4, 2 * core + x % 2)
                    route.append((src, device(y, core, z, x)))
    return route


def split(value):
    high = value.astype(BF16)
    return high, (value - high.astype(F32)).astype(BF16)


def pair_kernel(meta, own_pts, near_pts, far_pts, src, *refs, cut, turned):
    pieces = HEIGHT // cut
    outs, refs = (refs[:pieces], refs[pieces:]) if turned else ((), refs)
    out, high_t, low_t, high_w, low_w, buf, left, sem = refs[:8]

    def visit(slot, outer):
        @pl.when(meta[slot, 0] >= 0)
        def _():
            row_id = meta[slot, 0]
            col_id = meta[slot, 1]
            pick = row_id if turned else col_id
            copy = pltpu.make_async_copy(src.at[pick], buf, sem)
            copy.start()
            row_half = row_id // COL_CL
            row_k = row_id % COL_CL
            from_near = row_half == meta[SLOTS, 0]

            def row_line(c):
                a = near_pts[c, pl.ds(row_k, 1), :]
                b = far_pts[c, pl.ds(row_k, 1), :]
                return jnp.where(from_near, a, b)

            rows = [row_line(c) for c in range(4)]
            cols = [own_pts[c, pl.ds(col_id, 1), :] for c in range(4)]
            down, across = (cols, rows) if turned else (rows, cols)
            for c in range(4):
                left[c] = jnp.transpose(jnp.broadcast_to(down[c], (ZC, ZC)))

            def chunk(step, carry):
                at = pl.multiple_of(step * 16, 16)
                wide = [jnp.broadcast_to(v, (16, ZC)) for v in across]
                tall = [left[c, pl.ds(at, 16), :] for c in range(4)]
                dx = tall[0] - wide[0]
                dy = tall[1] - wide[1]
                dz = tall[2] - wide[2]
                inv = lax.rsqrt(dx * dx + dy * dy + dz * dz + 1.0)
                w = (COUPLE * (inv * inv * inv)) * (tall[3] * wide[3])
                nx, ny, nz = dx * inv, dy * inv, dz * inv
                u = [
                    nx * nx,
                    ny * ny,
                    nz * nz,
                    ROOT_TWO * (ny * nz),
                    ROOT_TWO * (nx * nz),
                    ROOT_TWO * (nx * ny),
                ]
                v = [w * t for t in u]
                v5 = [5.0 * t for t in v]
                for p in range(6):
                    for q in range(p, 6):
                        m = -(v5[p] * u[q])
                        if q < 3:
                            m = m + (v[p] + v[q])
                        elif p < 3:
                            m = m + v[q]
                        if p == q:
                            m = m + w
                        hi, lo = split(m)
                        high_t[pl.ds(p * ZC + at, 16), q * ZC : (q + 1) * ZC] = hi
                        low_t[pl.ds(p * ZC + at, 16), q * ZC : (q + 1) * ZC] = lo
                        if p != q:
                            high_t[pl.ds(q * ZC + at, 16), p * ZC : (p + 1) * ZC] = hi
                            low_t[pl.ds(q * ZC + at, 16), p * ZC : (p + 1) * ZC] = lo
                return carry

            lax.fori_loop(0, ZC // 16, chunk, 0)
            copy.wait()
            hi, lo = split(buf[...])
            high_w[...] = hi
            low_w[...] = lo
            step_rows = cut * 2

            def rows_of(g, carry):
                part = pl.ds(pl.multiple_of(g * step_rows, step_rows), step_rows)
                acc = jnp.dot(high_t[part, :], high_w[...], preferred_element_type=F32)
                acc += jnp.dot(high_t[part, :], low_w[...], preferred_element_type=F32)
                acc += jnp.dot(low_t[part, :], high_w[...], preferred_element_type=F32)
                for h in range(2):
                    out[(2 * g + h) ^ meta[SLOTS, 1], pl.ds(pl.multiple_of(slot * cut, cut), cut), :] = acc[h * cut : (h + 1) * cut]
                return carry

            lax.fori_loop(0, HEIGHT // step_rows, rows_of, 0)

        return outer

    lax.fori_loop(0, SLOTS, visit, 0)
    for slot in range(SLOTS):
        tag = jnp.full((1, 1, SK), meta[slot, 1 if turned else 0].astype(F32))
        out[:, SLOTS * cut + slot * (TAG // SLOTS) : SLOTS * cut + (slot + 1) * (TAG // SLOTS), :] = (
            jnp.broadcast_to(tag, (pieces, TAG // SLOTS, SK))
        )
    send_out(out, outs, refs[8:])


def send_out(held, outs, sems):
    copies = [pltpu.make_async_copy(held.at[k], one.at[0], sems[0].at[k]) for k, one in enumerate(outs)]
    for copy in copies:
        copy.start()
    for copy in copies:
        copy.wait()


def pair_terms(meta, own_pts, near_pts, far_pts, src, cut, turned):
    pieces = HEIGHT // cut
    vmem = pl.BlockSpec(memory_space=pltpu.VMEM)
    rows = SLOTS * cut + TAG
    if turned:
        shape = tuple(jax.ShapeDtypeStruct((1, rows, SK), F32) for _ in range(pieces))
        specs = tuple(pl.BlockSpec(memory_space=pltpu.HBM) for _ in range(pieces))
        held, sems = [pltpu.VMEM((pieces, rows, SK), F32)], [pltpu.SemaphoreType.DMA((pieces,))]
    else:
        shape, specs, held, sems = jax.ShapeDtypeStruct((pieces, rows, SK), F32), vmem, [], []
    return pl.pallas_call(
        functools.partial(pair_kernel, cut=cut, turned=turned),
        out_shape=shape,
        in_specs=[pl.BlockSpec(memory_space=pltpu.SMEM), vmem, vmem, vmem, pl.BlockSpec(memory_space=pltpu.HBM)],
        out_specs=specs,
        scratch_shapes=held
        + [
            pltpu.VMEM((HEIGHT, HEIGHT), BF16),
            pltpu.VMEM((HEIGHT, HEIGHT), BF16),
            pltpu.VMEM((HEIGHT, SK), BF16),
            pltpu.VMEM((HEIGHT, SK), BF16),
            pltpu.VMEM((HEIGHT, SK), F32),
            pltpu.VMEM((4, ZC, ZC), F32),
            pltpu.SemaphoreType.DMA,
        ]
        + sems,
        cost_estimate=pl.CostEstimate(flops=2_000_000_000, bytes_accessed=4_000_000, transcendentals=32768),
        name="pair_cols" if turned else "pair_rows",
    )(meta, own_pts, near_pts, far_pts, src)


def add_rows_kernel(ids, arrived, out, stage, sems, *, cut):
    total = ids.shape[0] * SLOTS

    def fetch(at, n):
        k, slot = n // SLOTS, n % SLOTS
        src = arrived.at[k, pl.ds(slot * cut, cut)]
        return pltpu.make_async_copy(src, stage.at[at], sems.at[at])

    for n in range(total):

        @pl.when(ids[n // SLOTS, n % SLOTS] >= 0)
        def _(n=n):
            fetch(n, n).start()

    out[...] = jnp.zeros_like(out)
    for n in range(total):

        @pl.when(ids[n // SLOTS, n % SLOTS] >= 0)
        def _(n=n):
            fetch(n, n).wait()
            out[ids[n // SLOTS, n % SLOTS]] += stage[n]


def add_rows(arrived, clusters, cut):
    ids = arrived[:, SLOTS * cut :: TAG // SLOTS, 0].astype(jnp.int32)
    total = ids.shape[0] * SLOTS
    return pl.pallas_call(
        functools.partial(add_rows_kernel, cut=cut),
        out_shape=jax.ShapeDtypeStruct((clusters, cut, SK), F32),
        in_specs=[pl.BlockSpec(memory_space=pltpu.SMEM), pl.BlockSpec(memory_space=pltpu.HBM)],
        out_specs=pl.BlockSpec(memory_space=pltpu.VMEM),
        scratch_shapes=[pltpu.VMEM((total, cut, SK), F32), pltpu.SemaphoreType.DMA((total,))],
        cost_estimate=pl.CostEstimate(flops=1_000_000, bytes_accessed=3_000_000, transcendentals=0),
        name="add_rows",
    )(ids, arrived)


def add_kernel(turn, *refs, cut, parts):
    arrived, outs, refs = refs[:parts], refs[parts : 2 * parts], refs[2 * parts :]
    if parts == 1:
        outs, refs = (), outs + refs
    out, stage, sems = refs[:3]
    total = stage.shape[0]
    copies = [
        pltpu.make_async_copy(arrived[0].at[k] if parts == 1 else arrived[k].at[0], stage.at[k], sems.at[k])
        for k in range(total)
    ]
    for copy in copies:
        copy.start()
    out[...] = jnp.zeros_like(out)
    for k in range(total):
        copies[k].wait()
        tags = stage[k, SLOTS * cut : SLOTS * cut + TAG, :128]
        for slot in range(SLOTS):
            pick = jnp.max(tags[slot * (TAG // SLOTS) : (slot + 1) * (TAG // SLOTS)]).astype(jnp.int32)

            @pl.when(pick >= 0)
            def _(k=k, slot=slot, pick=pick):
                out[pick ^ turn[0]] += stage[k, slot * cut : (slot + 1) * cut, :]

    send_out(out, outs, refs[3:])


def add_arrived(arrived, turn, clusters, cut):
    total = sum(part.shape[0] for part in arrived)
    smem = pl.BlockSpec(memory_space=pltpu.SMEM)
    if len(arrived) > 1:
        shape = tuple(jax.ShapeDtypeStruct((1, cut, SK), F32) for _ in range(clusters))
        specs = tuple(pl.BlockSpec(memory_space=pltpu.HBM) for _ in range(clusters))
        held, sems = [pltpu.VMEM((clusters, cut, SK), F32)], [pltpu.SemaphoreType.DMA((clusters,))]
    else:
        shape, held, sems = jax.ShapeDtypeStruct((clusters, cut, SK), F32), [], []
        specs = pl.BlockSpec(memory_space=pltpu.VMEM)
    return pl.pallas_call(
        functools.partial(add_kernel, cut=cut, parts=len(arrived)),
        out_shape=shape,
        in_specs=[smem] + [pl.BlockSpec(memory_space=pltpu.HBM)] * len(arrived),
        out_specs=specs,
        scratch_shapes=held
        + [pltpu.VMEM((total, SLOTS * cut + TAG, SK), F32), pltpu.SemaphoreType.DMA((total,))]
        + sems,
        cost_estimate=pl.CostEstimate(flops=1_000_000, bytes_accessed=3_000_000, transcendentals=0),
        name="add_arrived",
    )(turn.reshape(1), *arrived)


BLK = 64


def spread_lane(value, lane):
    return jnp.broadcast_to(value[:, lane : lane + 1], (8, 128))


def factor_inverse(diag, held):
    sub = lax.broadcasted_iota(jnp.int32, (8, 128), 0)
    lane = lax.broadcasted_iota(jnp.int32, (8, 128), 1)
    body = jnp.concatenate([diag, diag], axis=1)
    groups = []
    for g in range(BLK // 8):
        eye = jnp.where(lane == sub + 8 * g, 1.0, 0.0).astype(F32)
        groups.append(jnp.where(lane < BLK, eye, body[8 * g : 8 * g + 8]))
    done = []
    for kb in range(BLK // 8):
        at = BLK + 8 * kb
        spread = {
            g: [spread_lane(groups[g], at + t) for t in range(8)]
            for g in range(kb + 1, BLK // 8)
        }
        rows = [jnp.broadcast_to(groups[kb][t : t + 1, :], (8, 128)) for t in range(8)]
        for t in range(8):
            held[kb, t] = spread_lane(groups[kb], at + t)
        e = [
            [jnp.broadcast_to(held[kb, t, r : r + 1, :], (8, 128)) if r >= t else None for t in range(8)]
            for r in range(8)
        ]
        final = jnp.zeros((8, 128), F32)
        scaled = []
        m = {}
        for t in range(8):
            root = lax.rsqrt(e[t][t])
            inv = 1.0 / e[t][t]
            final = jnp.where(sub == t, rows[t] * root, final)
            scaled.append(rows[t] * inv)
            for r in range(t + 1, 8):
                m[r, t] = e[r][t] * inv
                for u in range(t + 1, r + 1):
                    e[r][u] = e[r][u] - m[r, t] * e[u][t]
                rows[r] = rows[r] - e[r][t] * scaled[t]
        for t in range(6, -1, -1):
            for r in range(7, t, -1):
                scaled[t] = scaled[t] - m[r, t] * scaled[r]
        for g in range(kb + 1, BLK // 8):
            for t in range(8):
                groups[g] = groups[g] - spread[g][t] * scaled[t]
        done.append(final)
    return jnp.concatenate(done, axis=0)[:, :BLK]


def basis_kernel(turn, rows, self_high, self_low, self_cols, *refs):
    cols = refs[:NR]
    out_rows, out_cols = refs[NR], refs[NR + 1 : 2 * NR + 1]
    sk, sk_high, sk_low, gram, inverse, low_q, pivots = refs[2 * NR + 1 :]
    n = SK // BLK
    dims0 = (((0,), (0,)), ((), ()))
    half = HEIGHT // 2
    sk[0, :half] = rows[:half] + self_high[...]
    sk[0, half:] = rows[half:] + self_low[...]
    for k in range(NR):
        part = pl.ds(pl.multiple_of((k ^ turn[0]) * COL_CUT, COL_CUT), COL_CUT)
        sk[1, part, :] = cols[k][0] + self_cols[part, :]
    for w in range(2):
        hi, lo = split(sk[w])
        sk_high[w] = hi
        sk_low[w] = lo
        cross = lax.dot_general(sk_high[w], sk_low[w], dims0, preferred_element_type=F32)
        gram[w] = lax.dot_general(sk_high[w], sk_high[w], dims0, preferred_element_type=F32) + (cross + cross.T)
        inverse[w] = jnp.zeros((SK, SK), F32)
    for k in range(n):
        here = slice(k * BLK, (k + 1) * BLK)
        low = [factor_inverse(gram[w, here, here], pivots.at[w]) for w in range(2)]
        for w in range(2):
            if k:
                inverse[w, here, : k * BLK] = jnp.dot(
                    low[w], inverse[w, here, : k * BLK], precision=HIGH, preferred_element_type=F32
                )
            inverse[w, here, here] = low[w]
            if k < n - 1:
                rest = slice((k + 1) * BLK, SK)
                upper = jnp.dot(low[w], gram[w, here, rest], precision=HIGH, preferred_element_type=F32)
                gram[w, rest, rest] = gram[w, rest, rest] - lax.dot_general(
                    upper, upper, dims0, precision=HIGH, preferred_element_type=F32
                )
                inverse[w, rest, : (k + 1) * BLK] = inverse[w, rest, : (k + 1) * BLK] - lax.dot_general(
                    upper, inverse[w, here, : (k + 1) * BLK], dims0, precision=HIGH, preferred_element_type=F32
                )
    dims1 = (((1,), (1,)), ((), ()))

    def product(w):
        hi, lo = split(inverse[w])
        q = lax.dot_general(sk_high[w], hi, dims1, preferred_element_type=F32)
        q += lax.dot_general(sk_high[w], lo, dims1, preferred_element_type=F32)
        return q + lax.dot_general(sk_low[w], hi, dims1, preferred_element_type=F32)

    q = product(1)
    for g in range(NR):
        low_q[g ^ turn[0]] = q[g * COL_CUT : (g + 1) * COL_CUT]
    for k in range(NR):
        out_cols[k][0] = low_q[k]
    out_rows[...] = product(0)


def bases(turn, rows, self_rows, cols, self_cols):
    shape = jax.ShapeDtypeStruct((HEIGHT, SK), F32)
    shape_c = jax.ShapeDtypeStruct((1, COL_CUT, SK), F32)
    vmem = pl.BlockSpec(memory_space=pltpu.VMEM)
    return pl.pallas_call(
        basis_kernel,
        out_shape=(shape,) + (shape_c,) * NR,
        in_specs=[pl.BlockSpec(memory_space=pltpu.SMEM)] + [vmem] * (4 + NR),
        out_specs=(vmem,) * (NR + 1),
        scratch_shapes=[
            pltpu.VMEM((2, HEIGHT, SK), F32),
            pltpu.VMEM((2, HEIGHT, SK), BF16),
            pltpu.VMEM((2, HEIGHT, SK), BF16),
            pltpu.VMEM((2, SK, SK), F32),
            pltpu.VMEM((2, SK, SK), F32),
            pltpu.VMEM((NR, COL_CUT, SK), F32),
            pltpu.VMEM((2, BLK // 8, 8, 8, 128), F32),
        ],
        compiler_params=pltpu.CompilerParams(vmem_limit_bytes=32 << 20),
        cost_estimate=pl.CostEstimate(flops=3_000_000_000, bytes_accessed=5_000_000, transcendentals=0),
        name="bases",
    )(turn.reshape(1), rows, *self_rows, self_cols, *cols)


def trade(value, axis):
    return lax.all_to_all(value, axis, split_axis=0, concat_axis=0, tiled=True)


def swap_rows(value):
    got = [value[0]]
    for k in range(1, NR):
        got.append(lax.ppermute(value[k], "row", [(i, i ^ k) for i in range(NR)]))
    return got


def level(positions, modulus, self_weight, omega, psi, blocks):
    row_at = lax.axis_index("row")
    col_at = lax.axis_index("col")
    near_route, far_route = point_routes()

    points = jnp.concatenate([positions, modulus[None]], axis=0).reshape(4, COL_CL, ZC)
    near_pts = lax.ppermute(points, BOTH, near_route)
    far_pts = lax.ppermute(points, BOTH, far_route)

    src_y, src_core, src_z, src_x = row_at // 2, row_at % 2, col_at // 4, col_at % 4
    bits = src_z ^ src_y
    omega_pick = (bits % 2) * 4 + (bits // 2) * 2 + ((src_x // 2) ^ src_core)
    half = HEIGHT // 2
    self_rows = []
    for h, turn in enumerate((0, 2)):
        inside, along = omega_routes(turn)
        pick = omega_pick ^ turn
        weight = lax.dynamic_slice(self_weight, (pick, h * half), (1, half)).reshape(half, 1)
        part = lax.dynamic_slice(omega, (pick, h * half, 0), (1, half, SK)).reshape(half, SK) * weight
        part = lax.ppermute(part, BOTH, inside)
        self_rows.append(lax.ppermute(part, BOTH, along))
    psi_pick = (src_x % 2) * 8 + ((src_z - src_y) % 4) * 2 + src_x // 2
    psi_here = lax.ppermute(psi[psi_pick], BOTH, psi_route())
    self_cols = psi_here * self_weight[row_at][:, None]

    pairs = blocks.reshape(SLOTS, 2)
    away = ((col_at % 4) // 2) ^ (row_at % 2)
    near_half = (col_at % 2) ^ away
    none = jnp.int32(0)
    row_meta = jnp.concatenate([pairs, jnp.stack([near_half, none])[None]], axis=0).astype(jnp.int32)
    col_meta = jnp.concatenate([pairs, jnp.stack([near_half, row_at])[None]], axis=0).astype(jnp.int32)

    row_terms = pair_terms(row_meta, points, near_pts, far_pts, omega, ROW_CUT, False)
    col_terms = pair_terms(col_meta, points, near_pts, far_pts, psi, COL_CUT, True)

    row_got = trade(row_terms, "col")
    col_got = swap_rows(col_terms)
    row_sum = add_rows(row_got, ROW_CL, ROW_CUT)
    col_sum = add_arrived(col_got, row_at, COL_CL, COL_CUT)
    rows = trade(row_sum, "col").reshape(HEIGHT, SK)
    cols = swap_rows(col_sum)
    row_q, *col_q = bases(row_at, rows, self_rows, cols, self_cols)
    row_basis = trade(row_q.reshape(NC, ROW_CUT, SK), "col")
    col_basis = jnp.zeros((NR, COL_CUT, SK), F32)
    for k, part in enumerate(swap_rows(col_q)):
        col_basis = lax.dynamic_update_slice_in_dim(col_basis, part, row_at ^ k, 0)
    return (row_basis, col_basis)


def solution(mesh):
    placed = (
        P(None, "col"),
        P("col"),
        P("col", None),
        P("col", None, None),
        P("row", None, None),
        P("row", "col", None, None),
    )
    return jax.shard_map(
        level,
        mesh=mesh,
        in_specs=placed,
        out_specs=(P("row", "col", None), P("col", "row", None)),
        check_vma=False,
    )
```

```python
import functools
import jax
import jax.numpy as jnp
from jax import lax
from jax.experimental import pallas as pl
from jax.experimental.pallas import tpu as pltpu
from jax.sharding import PartitionSpec as P

COUPLE = 0.25
ROOT_TWO = 1.4142135623730951
HIGH = lax.Precision.HIGHEST
ZC = 128
HEIGHT = 768
SK = 256
NR = 8
NC = 16
ROW_CL = 16
COL_CL = 8
SLOTS = 2
ROW_CUT = HEIGHT // NC
COL_CUT = HEIGHT // NR
TAG = 8
ORDER = (4, 5, 6, 7, 2, 3, 1)
BOTH = ("row", "col")
F32 = jnp.float32
BF16 = jnp.bfloat16


def device(y, core, z, x):
    return (2 * y + core) * NC + 4 * z + x


def point_routes():
    near, far = [], []
    for y in range(4):
        for core in range(2):
            for z in range(4):
                for x in range(4):
                    away = (x // 2) ^ core
                    bit = x % 2
                    target = device(y, core, z, x)
                    first = 2 * core + (bit ^ away)
                    second = 2 * core + (1 ^ bit ^ away)
                    src_y = (z + 2) % 4
                    near.append((device(src_y, away, y, first), target))
                    far.append((device(src_y, away, y, second), target))
    return near, far


def omega_routes(turn):
    inside, along = [], []
    for y in range(4):
        for core in range(2):
            for z in range(4):
                for x in range(4):
                    src_y = y ^ (2 * (x // 2) + z % 2) ^ turn
                    src_core = core ^ (x % 2)
                    middle = device(src_y, src_core, z, x)
                    inside.append((device(src_y, src_core, y, 2 * core + z // 2), middle))
                    along.append((middle, device(y, core, z, x)))
    return inside, along


def psi_route():
    route = []
    for y in range(4):
        for core in range(2):
            for z in range(4):
                for x in range(4):
                    src = device(z, x // 2, (y + z) % 4, 2 * core + x % 2)
                    route.append((src, device(y, core, z, x)))
    return route


def split(value):
    high = value.astype(BF16)
    return high, (value - high.astype(F32)).astype(BF16)


def pair_kernel(meta, own_pts, near_pts, far_pts, src, *refs, cut, turned):
    pieces = HEIGHT // cut
    outs, refs = (refs[:pieces], refs[pieces:]) if turned else ((), refs)
    out, high_t, low_t, high_w, low_w, buf, left, sem = refs[:8]

    def visit(slot, outer):
        @pl.when(meta[slot, 0] >= 0)
        def _():
            row_id = meta[slot, 0]
            col_id = meta[slot, 1]
            pick = row_id if turned else col_id
            copy = pltpu.make_async_copy(src.at[pick], buf, sem)
            copy.start()
            row_half = row_id // COL_CL
            row_k = row_id % COL_CL
            from_near = row_half == meta[SLOTS, 0]

            def row_line(c):
                a = near_pts[c, pl.ds(row_k, 1), :]
                b = far_pts[c, pl.ds(row_k, 1), :]
                return jnp.where(from_near, a, b)

            rows = [row_line(c) for c in range(4)]
            cols = [own_pts[c, pl.ds(col_id, 1), :] for c in range(4)]
            down, across = (cols, rows) if turned else (rows, cols)
            for c in range(4):
                left[c] = jnp.transpose(jnp.broadcast_to(down[c], (ZC, ZC)))

            def chunk(step, carry):
                at = pl.multiple_of(step * 16, 16)
                wide = [jnp.broadcast_to(v, (16, ZC)) for v in across]
                tall = [left[c, pl.ds(at, 16), :] for c in range(4)]
                dx = tall[0] - wide[0]
                dy = tall[1] - wide[1]
                dz = tall[2] - wide[2]
                inv = lax.rsqrt(dx * dx + dy * dy + dz * dz + 1.0)
                w = (COUPLE * (inv * inv * inv)) * (tall[3] * wide[3])
                nx, ny, nz = dx * inv, dy * inv, dz * inv
                u = [
                    nx * nx,
                    ny * ny,
                    nz * nz,
                    ROOT_TWO * (ny * nz),
                    ROOT_TWO * (nx * nz),
                    ROOT_TWO * (nx * ny),
                ]
                v = [w * t for t in u]
                v5 = [5.0 * t for t in v]
                for p in range(6):
                    for q in range(p, 6):
                        m = -(v5[p] * u[q])
                        if q < 3:
                            m = m + (v[p] + v[q])
                        elif p < 3:
                            m = m + v[q]
                        if p == q:
                            m = m + w
                        hi, lo = split(m)
                        high_t[pl.ds(p * ZC + at, 16), q * ZC : (q + 1) * ZC] = hi
                        low_t[pl.ds(p * ZC + at, 16), q * ZC : (q + 1) * ZC] = lo
                        if p != q:
                            high_t[pl.ds(q * ZC + at, 16), p * ZC : (p + 1) * ZC] = hi
                            low_t[pl.ds(q * ZC + at, 16), p * ZC : (p + 1) * ZC] = lo
                return carry

            lax.fori_loop(0, ZC // 16, chunk, 0)
            copy.wait()
            hi, lo = split(buf[...])
            high_w[...] = hi
            low_w[...] = lo
            step_rows = cut * 2

            def rows_of(g, carry):
                part = pl.ds(pl.multiple_of(g * step_rows, step_rows), step_rows)
                acc = jnp.dot(high_t[part, :], high_w[...], preferred_element_type=F32)
                acc += jnp.dot(high_t[part, :], low_w[...], preferred_element_type=F32)
                acc += jnp.dot(low_t[part, :], high_w[...], preferred_element_type=F32)
                for h in range(2):
                    out[(2 * g + h) ^ meta[SLOTS, 1], pl.ds(pl.multiple_of(slot * cut, cut), cut), :] = acc[h * cut : (h + 1) * cut]
                return carry

            lax.fori_loop(0, HEIGHT // step_rows, rows_of, 0)

        return outer

    lax.fori_loop(0, SLOTS, visit, 0)
    for slot in range(SLOTS):
        tag = jnp.full((1, 1, SK), meta[slot, 1 if turned else 0].astype(F32))
        out[:, SLOTS * cut + slot * (TAG // SLOTS) : SLOTS * cut + (slot + 1) * (TAG // SLOTS), :] = (
            jnp.broadcast_to(tag, (pieces, TAG // SLOTS, SK))
        )
    send_out(out, outs, refs[8:])


def send_out(held, outs, sems):
    copies = [pltpu.make_async_copy(held.at[k], one.at[0], sems[0].at[k]) for k, one in enumerate(outs)]
    for copy in copies:
        copy.start()
    for copy in copies:
        copy.wait()


def pair_terms(meta, own_pts, near_pts, far_pts, src, cut, turned):
    pieces = HEIGHT // cut
    vmem = pl.BlockSpec(memory_space=pltpu.VMEM)
    rows = SLOTS * cut + TAG
    if turned:
        shape = tuple(jax.ShapeDtypeStruct((1, rows, SK), F32) for _ in range(pieces))
        specs = tuple(pl.BlockSpec(memory_space=pltpu.HBM) for _ in range(pieces))
        held, sems = [pltpu.VMEM((pieces, rows, SK), F32)], [pltpu.SemaphoreType.DMA((pieces,))]
    else:
        shape, specs, held, sems = jax.ShapeDtypeStruct((pieces, rows, SK), F32), vmem, [], []
    return pl.pallas_call(
        functools.partial(pair_kernel, cut=cut, turned=turned),
        out_shape=shape,
        in_specs=[pl.BlockSpec(memory_space=pltpu.SMEM), vmem, vmem, vmem, pl.BlockSpec(memory_space=pltpu.HBM)],
        out_specs=specs,
        scratch_shapes=held
        + [
            pltpu.VMEM((HEIGHT, HEIGHT), BF16),
            pltpu.VMEM((HEIGHT, HEIGHT), BF16),
            pltpu.VMEM((HEIGHT, SK), BF16),
            pltpu.VMEM((HEIGHT, SK), BF16),
            pltpu.VMEM((HEIGHT, SK), F32),
            pltpu.VMEM((4, ZC, ZC), F32),
            pltpu.SemaphoreType.DMA,
        ]
        + sems,
        cost_estimate=pl.CostEstimate(flops=2_000_000_000, bytes_accessed=4_000_000, transcendentals=32768),
        name="pair_cols" if turned else "pair_rows",
    )(meta, own_pts, near_pts, far_pts, src)


def add_rows_kernel(ids, arrived, out, stage, sems, *, cut):
    total = ids.shape[0] * SLOTS

    def fetch(at, n):
        k, slot = n // SLOTS, n % SLOTS
        src = arrived.at[k, pl.ds(slot * cut, cut)]
        return pltpu.make_async_copy(src, stage.at[at], sems.at[at])

    for n in range(total):

        @pl.when(ids[n // SLOTS, n % SLOTS] >= 0)
        def _(n=n):
            fetch(n, n).start()

    out[...] = jnp.zeros_like(out)
    for n in range(total):

        @pl.when(ids[n // SLOTS, n % SLOTS] >= 0)
        def _(n=n):
            fetch(n, n).wait()
            out[ids[n // SLOTS, n % SLOTS]] += stage[n]


def add_rows(arrived, clusters, cut):
    ids = arrived[:, SLOTS * cut :: TAG // SLOTS, 0].astype(jnp.int32)
    total = ids.shape[0] * SLOTS
    return pl.pallas_call(
        functools.partial(add_rows_kernel, cut=cut),
        out_shape=jax.ShapeDtypeStruct((clusters, cut, SK), F32),
        in_specs=[pl.BlockSpec(memory_space=pltpu.SMEM), pl.BlockSpec(memory_space=pltpu.HBM)],
        out_specs=pl.BlockSpec(memory_space=pltpu.VMEM),
        scratch_shapes=[pltpu.VMEM((total, cut, SK), F32), pltpu.SemaphoreType.DMA((total,))],
        cost_estimate=pl.CostEstimate(flops=1_000_000, bytes_accessed=3_000_000, transcendentals=0),
        name="add_rows",
    )(ids, arrived)


def add_kernel(turn, *refs, cut, parts):
    arrived, outs, refs = refs[:parts], refs[parts : 2 * parts], refs[2 * parts :]
    if parts == 1:
        outs, refs = (), outs + refs
    out, stage, sems = refs[:3]
    total = stage.shape[0]
    copies = [
        pltpu.make_async_copy(arrived[0].at[k] if parts == 1 else arrived[k].at[0], stage.at[k], sems.at[k])
        for k in range(total)
    ]
    for copy in copies:
        copy.start()
    out[...] = jnp.zeros_like(out)
    for k in range(total):
        copies[k].wait()
        tags = stage[k, SLOTS * cut : SLOTS * cut + TAG, :128]
        for slot in range(SLOTS):
            pick = jnp.max(tags[slot * (TAG // SLOTS) : (slot + 1) * (TAG // SLOTS)]).astype(jnp.int32)

            @pl.when(pick >= 0)
            def _(k=k, slot=slot, pick=pick):
                out[pick ^ turn[0]] += stage[k, slot * cut : (slot + 1) * cut, :]

    send_out(out, outs, refs[3:])


def add_arrived(arrived, turn, clusters, cut):
    total = sum(part.shape[0] for part in arrived)
    smem = pl.BlockSpec(memory_space=pltpu.SMEM)
    if len(arrived) > 1:
        shape = tuple(jax.ShapeDtypeStruct((1, cut, SK), F32) for _ in range(clusters))
        specs = tuple(pl.BlockSpec(memory_space=pltpu.HBM) for _ in range(clusters))
        held, sems = [pltpu.VMEM((clusters, cut, SK), F32)], [pltpu.SemaphoreType.DMA((clusters,))]
    else:
        shape, held, sems = jax.ShapeDtypeStruct((clusters, cut, SK), F32), [], []
        specs = pl.BlockSpec(memory_space=pltpu.VMEM)
    return pl.pallas_call(
        functools.partial(add_kernel, cut=cut, parts=len(arrived)),
        out_shape=shape,
        in_specs=[smem] + [pl.BlockSpec(memory_space=pltpu.HBM)] * len(arrived),
        out_specs=specs,
        scratch_shapes=held
        + [pltpu.VMEM((total, SLOTS * cut + TAG, SK), F32), pltpu.SemaphoreType.DMA((total,))]
        + sems,
        cost_estimate=pl.CostEstimate(flops=1_000_000, bytes_accessed=3_000_000, transcendentals=0),
        name="add_arrived",
    )(turn.reshape(1), *arrived)


BLK = 64


def spread_lane(value, lane):
    return jnp.broadcast_to(value[:, lane : lane + 1], (8, 128))


def factor_inverse(diag, held):
    sub = lax.broadcasted_iota(jnp.int32, (8, 128), 0)
    lane = lax.broadcasted_iota(jnp.int32, (8, 128), 1)
    body = jnp.concatenate([diag, diag], axis=1)
    groups = []
    for g in range(BLK // 8):
        eye = jnp.where(lane == sub + 8 * g, 1.0, 0.0).astype(F32)
        groups.append(jnp.where(lane < BLK, eye, body[8 * g : 8 * g + 8]))
    done = []
    for kb in range(BLK // 8):
        at = BLK + 8 * kb
        spread = {
            g: [spread_lane(groups[g], at + t) for t in range(8)]
            for g in range(kb + 1, BLK // 8)
        }
        rows = [jnp.broadcast_to(groups[kb][t : t + 1, :], (8, 128)) for t in range(8)]
        for t in range(8):
            held[kb, t] = spread_lane(groups[kb], at + t)
        e = [
            [jnp.broadcast_to(held[kb, t, r : r + 1, :], (8, 128)) if r >= t else None for t in range(8)]
            for r in range(8)
        ]
        final = jnp.zeros((8, 128), F32)
        scaled = []
        m = {}
        for t in range(8):
            root = lax.rsqrt(e[t][t])
            inv = root * root
            final = jnp.where(sub == t, rows[t] * root, final)
            scaled.append(rows[t] * inv)
            for r in range(t + 1, 8):
                m[r, t] = e[r][t] * inv
                for u in range(t + 1, r + 1):
                    e[r][u] = e[r][u] - m[r, t] * e[u][t]
                rows[r] = rows[r] - e[r][t] * scaled[t]
        for t in range(6, -1, -1):
            for r in range(7, t, -1):
                scaled[t] = scaled[t] - m[r, t] * scaled[r]
        for g in range(kb + 1, BLK // 8):
            for t in range(8):
                groups[g] = groups[g] - spread[g][t] * scaled[t]
        done.append(final)
    return jnp.concatenate(done, axis=0)[:, :BLK]


def basis_kernel(turn, rows, self_high, self_low, self_cols, *refs):
    cols = refs[:NR]
    out_rows, out_cols = refs[NR], refs[NR + 1 : 2 * NR + 1]
    sk, sk_high, sk_low, gram, inverse, low_q, pivots = refs[2 * NR + 1 :]
    n = SK // BLK
    dims0 = (((0,), (0,)), ((), ()))
    half = HEIGHT // 2
    sk[0, :half] = rows[:half] + self_high[...]
    sk[0, half:] = rows[half:] + self_low[...]
    for k in range(NR):
        part = pl.ds(pl.multiple_of((k ^ turn[0]) * COL_CUT, COL_CUT), COL_CUT)
        sk[1, part, :] = cols[k][0] + self_cols[part, :]
    for w in range(2):
        hi, lo = split(sk[w])
        sk_high[w] = hi
        sk_low[w] = lo
        cross = lax.dot_general(sk_high[w], sk_low[w], dims0, preferred_element_type=F32)
        gram[w] = lax.dot_general(sk_high[w], sk_high[w], dims0, preferred_element_type=F32) + (cross + cross.T)
        inverse[w] = jnp.zeros((SK, SK), F32)
    for k in range(n):
        here = slice(k * BLK, (k + 1) * BLK)
        low = [factor_inverse(gram[w, here, here], pivots.at[w]) for w in range(2)]
        for w in range(2):
            if k:
                inverse[w, here, : k * BLK] = jnp.dot(
                    low[w], inverse[w, here, : k * BLK], precision=HIGH, preferred_element_type=F32
                )
            inverse[w, here, here] = low[w]
            if k < n - 1:
                rest = slice((k + 1) * BLK, SK)
                upper = jnp.dot(low[w], gram[w, here, rest], precision=HIGH, preferred_element_type=F32)
                gram[w, rest, rest] = gram[w, rest, rest] - lax.dot_general(
                    upper, upper, dims0, precision=HIGH, preferred_element_type=F32
                )
                inverse[w, rest, : (k + 1) * BLK] = inverse[w, rest, : (k + 1) * BLK] - lax.dot_general(
                    upper, inverse[w, here, : (k + 1) * BLK], dims0, precision=HIGH, preferred_element_type=F32
                )
    dims1 = (((1,), (1,)), ((), ()))

    def product(w):
        hi, lo = split(inverse[w])
        q = lax.dot_general(sk_high[w], hi, dims1, preferred_element_type=F32)
        q += lax.dot_general(sk_high[w], lo, dims1, preferred_element_type=F32)
        return q + lax.dot_general(sk_low[w], hi, dims1, preferred_element_type=F32)

    q = product(1)
    for g in range(NR):
        low_q[g ^ turn[0]] = q[g * COL_CUT : (g + 1) * COL_CUT]
    for k in range(NR):
        out_cols[k][0] = low_q[k]
    out_rows[...] = product(0)


def bases(turn, rows, self_rows, cols, self_cols):
    shape = jax.ShapeDtypeStruct((HEIGHT, SK), F32)
    shape_c = jax.ShapeDtypeStruct((1, COL_CUT, SK), F32)
    vmem = pl.BlockSpec(memory_space=pltpu.VMEM)
    return pl.pallas_call(
        basis_kernel,
        out_shape=(shape,) + (shape_c,) * NR,
        in_specs=[pl.BlockSpec(memory_space=pltpu.SMEM)] + [vmem] * (4 + NR),
        out_specs=(vmem,) * (NR + 1),
        scratch_shapes=[
            pltpu.VMEM((2, HEIGHT, SK), F32),
            pltpu.VMEM((2, HEIGHT, SK), BF16),
            pltpu.VMEM((2, HEIGHT, SK), BF16),
            pltpu.VMEM((2, SK, SK), F32),
            pltpu.VMEM((2, SK, SK), F32),
            pltpu.VMEM((NR, COL_CUT, SK), F32),
            pltpu.VMEM((2, BLK // 8, 8, 8, 128), F32),
        ],
        compiler_params=pltpu.CompilerParams(vmem_limit_bytes=32 << 20),
        cost_estimate=pl.CostEstimate(flops=3_000_000_000, bytes_accessed=5_000_000, transcendentals=0),
        name="bases",
    )(turn.reshape(1), rows, *self_rows, self_cols, *cols)


def trade(value, axis):
    return lax.all_to_all(value, axis, split_axis=0, concat_axis=0, tiled=True)


def swap_rows(value):
    got = {0: value[0]}
    for k in ORDER:
        got[k] = lax.ppermute(value[k], "row", [(i, i ^ k) for i in range(NR)])
    return [got[k] for k in range(NR)]


def level(positions, modulus, self_weight, omega, psi, blocks):
    row_at = lax.axis_index("row")
    col_at = lax.axis_index("col")
    near_route, far_route = point_routes()

    points = jnp.concatenate([positions, modulus[None]], axis=0).reshape(4, COL_CL, ZC)
    near_pts = lax.ppermute(points, BOTH, near_route)
    far_pts = lax.ppermute(points, BOTH, far_route)

    src_y, src_core, src_z, src_x = row_at // 2, row_at % 2, col_at // 4, col_at % 4
    bits = src_z ^ src_y
    omega_pick = (bits % 2) * 4 + (bits // 2) * 2 + ((src_x // 2) ^ src_core)
    half = HEIGHT // 2
    self_rows = []
    for h, turn in enumerate((0, 2)):
        inside, along = omega_routes(turn)
        pick = omega_pick ^ turn
        weight = lax.dynamic_slice(self_weight, (pick, h * half), (1, half)).reshape(half, 1)
        part = lax.dynamic_slice(omega, (pick, h * half, 0), (1, half, SK)).reshape(half, SK) * weight
        part = lax.ppermute(part, BOTH, inside)
        self_rows.append(lax.ppermute(part, BOTH, along))
    psi_pick = (src_x % 2) * 8 + ((src_z - src_y) % 4) * 2 + src_x // 2
    psi_here = lax.ppermute(psi[psi_pick], BOTH, psi_route())
    self_cols = psi_here * self_weight[row_at][:, None]

    pairs = blocks.reshape(SLOTS, 2)
    away = ((col_at % 4) // 2) ^ (row_at % 2)
    near_half = (col_at % 2) ^ away
    none = jnp.int32(0)
    row_meta = jnp.concatenate([pairs, jnp.stack([near_half, none])[None]], axis=0).astype(jnp.int32)
    col_meta = jnp.concatenate([pairs, jnp.stack([near_half, row_at])[None]], axis=0).astype(jnp.int32)

    row_terms = pair_terms(row_meta, points, near_pts, far_pts, omega, ROW_CUT, False)
    col_terms = pair_terms(col_meta, points, near_pts, far_pts, psi, COL_CUT, True)

    row_got = trade(row_terms, "col")
    col_got = swap_rows(col_terms)
    row_sum = add_rows(row_got, ROW_CL, ROW_CUT)
    col_sum = add_arrived(col_got, row_at, COL_CL, COL_CUT)
    rows = trade(row_sum, "col").reshape(HEIGHT, SK)
    cols = swap_rows(col_sum)
    row_q, *col_q = bases(row_at, rows, self_rows, cols, self_cols)
    row_basis = trade(row_q.reshape(NC, ROW_CUT, SK), "col")
    col_basis = jnp.zeros((NR, COL_CUT, SK), F32)
    for k, part in enumerate(swap_rows(col_q)):
        col_basis = lax.dynamic_update_slice_in_dim(col_basis, part, row_at ^ k, 0)
    return (row_basis, col_basis)


def solution(mesh):
    placed = (
        P(None, "col"),
        P("col"),
        P("col", None),
        P("col", None, None),
        P("row", None, None),
        P("row", "col", None, None),
    )
    return jax.shard_map(
        level,
        mesh=mesh,
        in_specs=placed,
        out_specs=(P("row", "col", None), P("col", "row", None)),
        check_vma=False,
    )
```
